256 devices in a mesh: dp: 8 (over z_hi, x), row: 4 (over y), col: 8 (over z_lo, core).
Axes of the slice: x: 4, y: 4, z: 8 (z_hi: 2, z_lo: 4; z = z_hi * 4 + z_lo), core: 2. Of those that a mesh axis runs over, the one named last changes fastest.
Arguments:
- acts: bfloat16 [4096, 8192], P(('dp', 'col'), 'row'), may hold values from -0.25 to 0.25
- grad_out: bfloat16 [4096, 14336], P(('dp', 'row'), 'col'), may hold values from -6 to 6
- weight: bfloat16 [8192, 14336], P('row', 'col'), may hold values from -0.0625 to 0.0625
Outputs:
- grad_input: bfloat16 [4096, 8192], P(('dp', 'col'), 'row')
- grad_weight: bfloat16 [4, 2048, 14336], P('row', 'dp', 'col')
The draws below stay inside these ranges and needn't reach their ends.
All inputs are finite; a program needn't handle non-finite values.
Results may differ from the reference program's by a relative error of at most 0.001.
Values may be sent and summed in bfloat16 or wider, within the bound.
A program may use at most 128 MiB of HBM per device.

```python
import jax
import jax.numpy as jnp

D = 8192
FF = 14336
FRAMES = 4096
N_ROW = 4


def strengthened(values, rng, source, target, shards_of, factor):
    owner, partner = [(jnp.arange(values.shape[axis_at]) // (values.shape[axis_at] // shards_of)).reshape([-1 if axis == axis_at else 1 for axis in range(values.ndim)]) for axis_at in (source, target)]
    chosen = jax.random.permutation(rng, shards_of)[partner]
    strong = (owner == chosen) | (owner == (partner + shards_of // 2) % shards_of)
    return jnp.where(strong, factor * values, values)


def shard_levels(stream_key, shape, split, smallest, largest):
    def one(position, shards_of):
        heights = jax.random.uniform(jax.random.fold_in(jax.random.fold_in(stream_key, 6), position), (shards_of,), jnp.float32, smallest / len(split), largest / len(split))
        return jnp.repeat(jnp.exp(heights), shape[position] // shards_of).reshape((-1,) + (1,) * (len(shape) - position - 1))

    factor_of = one(*split[0])
    for cut in split[1:]:
        factor_of = factor_of * one(*cut)
    return factor_of


def centred(stream_key, shape, spread, bound, cuts=(), held_as=jnp.bfloat16):
    gain = shard_levels(stream_key, shape, cuts, -0.22, 0.18) if cuts else 1.0
    values = jax.random.normal(stream_key, shape, jnp.float32) * spread * gain
    return jnp.minimum(jnp.maximum(values, -bound), bound).astype(held_as)


def noise_with(own_key, shape, spread, most, pieces, heavy, kind=jnp.bfloat16):
    values = spread * jax.random.normal(own_key, shape, jnp.float32)
    if pieces:
        values = values * shard_levels(own_key, shape, pieces, -0.22, 0.18)
    return jnp.clip(strengthened(values, jax.random.fold_in(own_key, 3), *heavy), -most, most).astype(kind)


def setup_inputs(seed: int = 0) -> dict:
    arg_keys = jax.random.split(jax.random.key(seed), 4)
    acts = centred(arg_keys[0], (FRAMES, D), (FRAMES ** -0.5), 0.25, ((0, 64), (1, 4)))
    grad_out = noise_with(arg_keys[1], (FRAMES, FF), 1.0, 6.0, ((0, 32), (1, 8)), (0, 1, 32, 2.75))
    weight = centred(arg_keys[2], (D, FF), D ** -0.5, 0.0625, ((0, 4), (1, 8)))
    return dict(acts=acts, grad_out=grad_out, weight=weight)


def reference(acts, grad_out, weight):
    grad_input = jnp.dot(grad_out, weight.T, preferred_element_type=jnp.float32).astype(jnp.bfloat16)
    full = jnp.dot(acts.T, grad_out, preferred_element_type=jnp.float32)
    grad_weight = full.astype(jnp.bfloat16).reshape(N_ROW, D // N_ROW, FF)
    return grad_input, grad_weight
```

```python
import functools

import jax
import jax.numpy as jnp
from jax import lax
from jax.experimental import pallas as pl
from jax.experimental.pallas import tpu as pltpu
from jax.sharding import PartitionSpec as P

MESH = pl.DeviceIdType.MESH
F32 = jnp.float32
BF16 = jnp.bfloat16
NX = NY = NL = 4
NH = 2
NZ = NH * NL
TILE = 256


class Ring:
    def __init__(self, slot, loc, me, n, dev, send_sem, recv_sem):
        self.slot, self.loc, self.dev = slot, loc, dev
        self.me = me
        self.left, self.right, self.far = (lax.rem(me + s, n) for s in (n - 1, 1, 2))
        self.sends, self.recvs = send_sem, recv_sem

    def _copy(self, ref, k, to):
        i = self.slot * 4 + k
        return pltpu.make_async_remote_copy(
            ref, ref, self.sends.at[i], self.recvs.at[i], device_id=self.dev(to), device_id_type=MESH
        )

    def _half(self, o, k):
        ref = self.loc(o)
        rows = ref.shape[0] // 2
        return ref.at[pl.ds(k * rows, rows)]

    def own(self):
        self._copy(self.loc(self.me), 0, self.right).start()
        self._copy(self.loc(self.me), 1, self.left).start()

    def from_left(self):
        self._copy(self.loc(self.left), 0, self.right).wait_recv()
        self._copy(self._half(self.left, 0), 2, self.right).start()

    def from_right(self):
        self._copy(self.loc(self.right), 1, self.left).wait_recv()
        self._copy(self._half(self.right, 1), 3, self.left).start()

    def from_far(self):
        self._copy(self._half(self.far, 0), 2, self.right).wait_recv()
        self._copy(self._half(self.far, 1), 3, self.left).wait_recv()

    def wait_sent(self):
        self._copy(self.loc(self.me), 0, self.right).wait_send()
        self._copy(self.loc(self.me), 1, self.left).wait_send()
        self._copy(self._half(self.left, 0), 2, self.right).wait_send()
        self._copy(self._half(self.right, 1), 3, self.left).wait_send()


def kernel(
    acts_hbm, grad_hbm, w_hbm, gi_ref, gw_ref,
    gp, gq, w, acts, xbuf, aall, at, acc, lhs, part, pair, near, mid,
    ring_send, ring_recv, loc_sem, hx_send, hx_recv, ax_send, ax_recv, az_send, az_recv,
    ac_send, ac_recv, pr_send, pr_recv, rs_send, rs_recv,
):
    dp, y, col = lax.axis_index("dp"), lax.axis_index("row"), lax.axis_index("col")
    h, x, l, c = dp // NX, dp % NX, col // 2, col % 2
    z = h * NL + l
    oh = 1 - h
    half = gp.shape[3]
    kb = acts.shape[1] // NZ
    nk = part.shape[4]

    def dev_x(to):
        return (h * NX + to, y, col)

    def dev_y(to):
        return (dp, to, col)

    def at_z(s):
        return lax.rem(z + s, NZ)

    def dev_z(s):
        to = at_z(s)
        return ((to // NL) * NX + x, y, (to % NL) * 2 + c)

    pal = (dp, y, l * 2 + 1 - c)

    own_p = pltpu.make_async_copy(grad_hbm.at[pl.ds(0, half)], gp.at[h, x, y], loc_sem.at[0])
    own_q = pltpu.make_async_copy(grad_hbm.at[pl.ds(half, half)], gq.at[h, y, x], loc_sem.at[1])
    own_a = pltpu.make_async_copy(acts_hbm, acts, loc_sem.at[2])
    own_w = pltpu.make_async_copy(w_hbm, w, loc_sem.at[3])
    own_a.start()
    own_p.start()
    own_q.start()
    own_w.start()

    barrier = pltpu.get_barrier_semaphore()
    peers = [dev_x(lax.rem(x + s, NX)) for s in range(1, NX)]
    peers += [dev_y(lax.rem(y + s, NY)) for s in (1, NY - 1)]
    peers += [dev_z(s) for s in range(1, NZ)] + [pal]
    for peer in peers:
        pl.semaphore_signal(barrier, inc=1, device_id=peer, device_id_type=MESH)
    own_a.wait()
    own_p.wait()
    own_q.wait()
    pl.semaphore_wait(barrier, len(peers))

    sent = []

    hx_p = pltpu.make_async_remote_copy(
        gp.at[h, x, y], gp.at[h, x, y], hx_send.at[0], hx_recv.at[0], device_id=dev_z(NL), device_id_type=MESH
    )
    hx_q = pltpu.make_async_remote_copy(
        gq.at[h, y, x], gq.at[h, y, x], hx_send.at[1], hx_recv.at[1], device_id=dev_z(NL), device_id_type=MESH
    )
    ax = []
    for s in range(1, NX):
        to = lax.rem(x + s, NX)
        for b in range(NH):
            i = (s - 1) * NH + b
            cols = pl.ds(pl.multiple_of((b * NX + to) * kb, kb), kb)
            cp = pltpu.make_async_remote_copy(
                acts.at[:, cols], xbuf.at[b, x], ax_send.at[i], ax_recv.at[i],
                device_id=dev_x(to), device_id_type=MESH,
            )
            cp.start()
            ax.append(cp)
    hx_p.start()
    hx_q.start()
    sent += ax + [hx_p, hx_q]
    for b in range(NH):
        cols = pl.ds(pl.multiple_of((b * NX + x) * kb, kb), kb)
        xbuf[b, x] = acts[:, cols]

    slot = iter(range(20))

    def ring(axis, loc):
        me, dev = (x, dev_x) if axis == "x" else (y, dev_y)
        return Ring(next(slot), loc, me, NX, dev, ring_send, ring_recv)

    def p1(b):
        return ring("x", lambda o: gp.at[b, o, y])

    def p2(b, i):
        return ring("y", lambda o: gp.at[b, i, o])

    def q1(b):
        return ring("y", lambda o: gq.at[b, o, x])

    def q2(b, i):
        return ring("x", lambda o: gq.at[b, i, o])

    xs = [x, lax.rem(x + NX - 1, NX), lax.rem(x + 1, NX), lax.rem(x + 2, NX)]
    ys = [y, lax.rem(y + NY - 1, NY), lax.rem(y + 1, NY), lax.rem(y + 2, NY)]
    pa, qa = [p1(h), p1(oh)], [q1(h), q1(oh)]
    pb = [[p2(b, i) for i in xs] for b in (h, oh)]
    qb = [[q2(b, i) for i in ys] for b in (h, oh)]

    acc[...] = jnp.zeros_like(acc)

    def group(is_p, b, i):
        if is_p:
            a = jnp.concatenate([aall[0, b * NL + j, i] for j in range(NY)], axis=0)
            g = gp.at[b, i]
        else:
            a = aall[1, b * NL + i].reshape(NX * half, kb)
            g = gq.at[b, i]
        at[...] = a.astype(F32).T.astype(BF16)

        @pl.loop(0, acc.shape[1] // TILE)
        def _(t):
            n = pl.ds(pl.multiple_of(t * TILE, TILE), TILE)
            acc[:, n] += jnp.dot(at[...], g[:, :, n].reshape(NX * half, TILE), preferred_element_type=F32)

    def lr(r):
        r.from_left()
        r.from_right()

    def grow(first, second):
        first.from_left()
        second[1].own()
        first.from_right()
        second[2].own()

    pa[0].own()
    qa[0].own()
    pb[0][0].own()
    qb[0][0].own()

    for cp in ax:
        cp.wait_recv()
    az = []
    for s in (1, NZ - 1, 2, NZ - 2, 3, NZ - 3, 4):
        b = at_z(s) // NL
        cp = pltpu.make_async_remote_copy(
            xbuf.at[b], aall.at[c, z], az_send.at[s - 1], az_recv.at[s - 1],
            device_id=dev_z(s), device_id_type=MESH,
        )
        cp.start()
        az.append(cp)
    aall[c, z] = xbuf[h]

    def to_pal(s):
        ref = aall.at[c, at_z(s)]
        return pltpu.make_async_remote_copy(
            ref, ref, ac_send.at[s], ac_recv.at[s], device_id=pal, device_id_type=MESH
        )

    def from_pal(s):
        ref = aall.at[1 - c, at_z(s)]
        return pltpu.make_async_remote_copy(
            ref, ref, ac_send.at[s], ac_recv.at[s], device_id=pal, device_id_type=MESH
        )

    to_pal(0).start()

    grow(pa[0], pb[0])
    grow(qa[0], qb[0])
    lr(pb[0][0])
    lr(qb[0][0])
    pa[0].from_far()
    pb[0][3].own()
    qa[0].from_far()
    qb[0][3].own()
    for i in (1, 2):
        lr(pb[0][i])
        lr(qb[0][i])
    hx_p.wait_recv()
    pa[1].own()
    pb[1][0].own()
    hx_q.wait_recv()
    qa[1].own()
    qb[1][0].own()
    lr(pb[0][3])
    lr(qb[0][3])

    for s in range(1, NZ):
        ref = aall.at[c, at_z(NZ - s)]
        pltpu.make_async_remote_copy(
            ref, ref, az_send.at[s - 1], az_recv.at[s - 1], device_id=dev_z(s), device_id_type=MESH
        ).wait_recv()
        to_pal(NZ - s).start()

    grow(pa[1], pb[1])
    grow(qa[1], qb[1])
    lr(pb[1][0])
    lr(qb[1][0])
    pa[1].from_far()
    pb[1][3].own()
    qa[1].from_far()
    qb[1][3].own()

    pb[0][0].from_far()
    pb[1][0].from_far()
    for d, s in enumerate((2, 0, 1, NZ - 1, NZ - 2)):
        to = at_z(s)
        lhs[0, d] = gp[to // NL, x, to % NL]
        lhs[1, d] = gq[to // NL, to % NL, x]
    own_w.wait()

    def partial(k):
        @pl.loop(0, nk // TILE)
        def _(t):
            cols = pl.ds(pl.multiple_of(t * TILE, TILE), TILE)
            rows = pl.ds(pl.multiple_of(k * nk + t * TILE, TILE), TILE)
            both = lhs[:, k : k + 4].reshape(8 * half, lhs.shape[3])
            r = lax.dot_general(both, w[rows], (((1,), (1,)), ((), ())), preferred_element_type=F32)
            part[:, k, :, :, cols] = r.reshape(2, 4, half, TILE)

    def pair_copy(k):
        return pltpu.make_async_remote_copy(
            part.at[1 - c, k], pair.at[k], pr_send.at[k], pr_recv.at[k], device_id=pal, device_id_type=MESH
        )

    def scatter(k):
        pair_copy(k).wait_recv()
        part[c, k] += pair[k]
        todo = (((0, 2, mid.at[0]), (2, 1, near.at[0, 0]), (3, NZ - 1, near.at[1, 0])) if k == 0 else
                ((3, NZ - 2, mid.at[1]), (1, 1, near.at[0, 1]), (2, NZ - 1, near.at[1, 1])))
        out = []
        for i, (d, s, dst) in enumerate(todo):
            cp = pltpu.make_async_remote_copy(
                part.at[c, k, d], dst, rs_send.at[k * 3 + i], rs_recv.at[k * 3 + i],
                device_id=dev_z(s), device_id_type=MESH,
            )
            cp.start()
            out.append(cp)
        return out

    partial(0)
    pair_copy(0).start()
    lr(pb[1][1])
    lr(qb[1][1])
    rs = scatter(0)
    partial(1)
    pair_copy(1).start()
    lr(pb[1][2])
    lr(qb[1][2])
    rs += scatter(1)

    for s in range(NZ):
        from_pal(s).wait_recv()
    for i in range(1, 4):
        pb[0][i].from_far()
    for i in range(4):
        qb[0][i].from_far()
        group(True, h, xs[i])
        if i == 1:
            lr(pb[1][3])
            lr(qb[1][3])
    for i in range(4):
        group(False, h, ys[i])
    for i in range(4):
        if i:
            pb[1][i].from_far()
        group(True, oh, xs[i])
        qb[1][i].from_far()
        group(False, oh, ys[i])

    for cp in rs:
        cp.wait_recv()
    gi_ref[:, :nk] = (part[c, 0, 1] + mid[0] + near[0, 0] + near[1, 0]).astype(BF16)
    gi_ref[:, nk:] = (part[c, 1, 0] + mid[1] + near[0, 1] + near[1, 1]).astype(BF16)
    gw_ref[0] = acc[...].astype(BF16)

    for r in pa + qa + pb[0] + pb[1] + qb[0] + qb[1]:
        r.wait_sent()
    for cp in sent + az + rs:
        cp.wait_send()
    for s in range(NZ):
        to_pal(s).wait_send()
    pair_copy(0).wait_send()
    pair_copy(1).wait_send()


def shards(acts, grad_out, weight):
    frames, width = acts.shape
    rows, hidden = grad_out.shape
    half = rows // 2
    kb = width // NZ
    nk = width // 2
    dma = pltpu.SemaphoreType.DMA
    return pl.pallas_call(
        kernel,
        out_shape=(
            jax.ShapeDtypeStruct((frames, width), BF16),
            jax.ShapeDtypeStruct((1, kb, hidden), BF16),
        ),
        in_specs=[pl.BlockSpec(memory_space=pl.ANY)] * 3,
        out_specs=(pl.BlockSpec(memory_space=pltpu.VMEM),) * 2,
        scratch_shapes=[
            pltpu.VMEM((NH, NX, NY, half, hidden), BF16),
            pltpu.VMEM((NH, NY, NX, half, hidden), BF16),
            pltpu.VMEM((width, hidden), BF16),
            pltpu.VMEM((frames, width), BF16),
            pltpu.VMEM((NH, NX, frames, kb), BF16),
            pltpu.VMEM((2, NZ, NX, frames, kb), BF16),
            pltpu.VMEM((kb, NX * half), BF16),
            pltpu.VMEM((kb, hidden), F32),
            pltpu.VMEM((2, 5, half, hidden), BF16),
            pltpu.VMEM((2, 2, 4, half, nk), F32),
            pltpu.VMEM((2, 4, half, nk), F32),
            pltpu.VMEM((2, 2, half, nk), F32),
            pltpu.VMEM((2, half, nk), F32),
            dma((80,)), dma((80,)), dma((4,)), dma((2,)), dma((2,)), dma((6,)), dma((6,)),
            dma((7,)), dma((7,)), dma((8,)), dma((8,)), dma((2,)), dma((2,)), dma((6,)), dma((6,)),
        ],
        compiler_params=pltpu.CompilerParams(
            collective_id=0, has_side_effects=True, vmem_limit_bytes=62 << 20
        ),
        name="grads",
    )(acts, grad_out, weight)


def solution(mesh):
    in_specs = (P(("dp", "col"), "row"), P(("dp", "row"), "col"), P("row", "col"))
    out_specs = (P(("dp", "col"), "row"), P("row", "dp", "col"))
    return jax.shard_map(shards, mesh=mesh, in_specs=in_specs, out_specs=out_specs, check_vma=False)
```

```python
import functools

import jax
import jax.numpy as jnp
from jax import lax
from jax.experimental import pallas as pl
from jax.experimental.pallas import tpu as pltpu
from jax.sharding import PartitionSpec as P

MESH = pl.DeviceIdType.MESH
F32 = jnp.float32
BF16 = jnp.bfloat16
NX = NY = NL = 4
NH = 2
NZ = NH * NL
TILE = 512


class Ring:
    def __init__(self, slot, loc, me, n, dev, send_sem, recv_sem):
        self.slot, self.loc, self.dev = slot, loc, dev
        self.me = me
        self.left, self.right, self.far = (lax.rem(me + s, n) for s in (n - 1, 1, 2))
        self.sends, self.recvs = send_sem, recv_sem

    def _copy(self, ref, k, to):
        i = self.slot * 4 + k
        return pltpu.make_async_remote_copy(
            ref, ref, self.sends.at[i], self.recvs.at[i], device_id=self.dev(to), device_id_type=MESH
        )

    def _half(self, o, k):
        ref = self.loc(o)
        rows = ref.shape[0] // 2
        return ref.at[pl.ds(k * rows, rows)]

    def own(self):
        self._copy(self.loc(self.me), 0, self.right).start()
        self._copy(self.loc(self.me), 1, self.left).start()

    def from_left(self):
        self._copy(self.loc(self.left), 0, self.right).wait_recv()
        self._copy(self._half(self.left, 0), 2, self.right).start()

    def from_right(self):
        self._copy(self.loc(self.right), 1, self.left).wait_recv()
        self._copy(self._half(self.right, 1), 3, self.left).start()

    def from_far(self):
        self._copy(self._half(self.far, 0), 2, self.right).wait_recv()
        self._copy(self._half(self.far, 1), 3, self.left).wait_recv()

    def wait_sent(self):
        self._copy(self.loc(self.me), 0, self.right).wait_send()
        self._copy(self.loc(self.me), 1, self.left).wait_send()
        self._copy(self._half(self.left, 0), 2, self.right).wait_send()
        self._copy(self._half(self.right, 1), 3, self.left).wait_send()


def kernel(
    acts_hbm, grad_hbm, w_hbm, gi_ref, gw_ref,
    gp, gq, w, acts, xbuf, aall, acc, lhs, part, pair, near, mid,
    ring_send, ring_recv, loc_sem, hx_send, hx_recv, ax_send, ax_recv, az_send, az_recv,
    ac_send, ac_recv, pr_send, pr_recv, rs_send, rs_recv,
):
    dp, y, col = lax.axis_index("dp"), lax.axis_index("row"), lax.axis_index("col")
    h, x, l, c = dp // NX, dp % NX, col // 2, col % 2
    z = h * NL + l
    oh = 1 - h
    half = gp.shape[3]
    kb = acts.shape[1] // NZ
    nk = part.shape[4]

    def dev_x(to):
        return (h * NX + to, y, col)

    def dev_y(to):
        return (dp, to, col)

    def at_z(s):
        return lax.rem(z + s, NZ)

    def dev_z(s):
        to = at_z(s)
        return ((to // NL) * NX + x, y, (to % NL) * 2 + c)

    pal = (dp, y, l * 2 + 1 - c)

    own_p = pltpu.make_async_copy(grad_hbm.at[pl.ds(0, half)], gp.at[h, x, y], loc_sem.at[0])
    own_q = pltpu.make_async_copy(grad_hbm.at[pl.ds(half, half)], gq.at[h, y, x], loc_sem.at[1])
    own_a = pltpu.make_async_copy(acts_hbm, acts, loc_sem.at[2])
    own_w = pltpu.make_async_copy(w_hbm, w, loc_sem.at[3])
    own_a.start()
    own_p.start()
    own_q.start()
    own_w.start()

    barrier = pltpu.get_barrier_semaphore()
    peers = [dev_x(lax.rem(x + s, NX)) for s in range(1, NX)]
    peers += [dev_y(lax.rem(y + s, NY)) for s in (1, NY - 1)]
    peers += [dev_z(s) for s in range(1, NZ)] + [pal]
    for peer in peers:
        pl.semaphore_signal(barrier, inc=1, device_id=peer, device_id_type=MESH)
    own_a.wait()
    own_p.wait()
    own_q.wait()
    pl.semaphore_wait(barrier, len(peers))

    sent = []

    hx_p = pltpu.make_async_remote_copy(
        gp.at[h, x, y], gp.at[h, x, y], hx_send.at[0], hx_recv.at[0], device_id=dev_z(NL), device_id_type=MESH
    )
    hx_q = pltpu.make_async_remote_copy(
        gq.at[h, y, x], gq.at[h, y, x], hx_send.at[1], hx_recv.at[1], device_id=dev_z(NL), device_id_type=MESH
    )
    ax = []
    for s in range(1, NX):
        to = lax.rem(x + s, NX)
        for b in range(NH):
            i = (s - 1) * NH + b
            cols = pl.ds(pl.multiple_of((b * NX + to) * kb, kb), kb)
            cp = pltpu.make_async_remote_copy(
                acts.at[:, cols], xbuf.at[b, x], ax_send.at[i], ax_recv.at[i],
                device_id=dev_x(to), device_id_type=MESH,
            )
            cp.start()
            ax.append(cp)
    hx_p.start()
    hx_q.start()
    sent += ax + [hx_p, hx_q]
    for b in range(NH):
        cols = pl.ds(pl.multiple_of((b * NX + x) * kb, kb), kb)
        xbuf[b, x] = acts[:, cols]

    slot = iter(range(20))

    def ring(axis, loc):
        me, dev = (x, dev_x) if axis == "x" else (y, dev_y)
        return Ring(next(slot), loc, me, NX, dev, ring_send, ring_recv)

    def p1(b):
        return ring("x", lambda o: gp.at[b, o, y])

    def p2(b, i):
        return ring("y", lambda o: gp.at[b, i, o])

    def q1(b):
        return ring("y", lambda o: gq.at[b, o, x])

    def q2(b, i):
        return ring("x", lambda o: gq.at[b, i, o])

    xs = [x, lax.rem(x + NX - 1, NX), lax.rem(x + 1, NX), lax.rem(x + 2, NX)]
    ys = [y, lax.rem(y + NY - 1, NY), lax.rem(y + 1, NY), lax.rem(y + 2, NY)]
    pa, qa = [p1(h), p1(oh)], [q1(h), q1(oh)]
    pb = [[p2(b, i) for i in xs] for b in (h, oh)]
    qb = [[q2(b, i) for i in ys] for b in (h, oh)]

    acc[...] = jnp.zeros_like(acc)
    wide = acc.shape[1] // 2

    def group(is_p, b, i):
        if is_p:
            a = jnp.concatenate([aall[0, b * NL + j, i] for j in range(NY)], axis=0)
            g = gp.at[b, i]
        else:
            a = aall[1, b * NL + i].reshape(NX * half, kb)
            g = gq.at[b, i]

        @pl.loop(0, acc.shape[1] // wide)
        def _(t):
            n = pl.ds(pl.multiple_of(t * wide, 128), wide)
            acc[:, n] += lax.dot_general(
                a, g[:, :, n].reshape(NX * half, wide), (((0,), (0,)), ((), ())), preferred_element_type=F32
            )

    def lr(r):
        r.from_left()
        r.from_right()

    def grow(first, second):
        first.from_left()
        second[1].own()
        first.from_right()
        second[2].own()

    az = []

    def acts_z():
        for cp in ax:
            cp.wait_recv()
        for s in (1, NZ - 1, 2, NZ - 2, 3, NZ - 3, 4):
            b = at_z(s) // NL
            cp = pltpu.make_async_remote_copy(
                xbuf.at[b], aall.at[c, z], az_send.at[s - 1], az_recv.at[s - 1],
                device_id=dev_z(s), device_id_type=MESH,
            )
            cp.start()
            az.append(cp)
        aall[c, z] = xbuf[h]
        to_pal(0).start()

    def to_pal(s):
        ref = aall.at[c, at_z(s)]
        return pltpu.make_async_remote_copy(
            ref, ref, ac_send.at[s], ac_recv.at[s], device_id=pal, device_id_type=MESH
        )

    def from_pal(s):
        ref = aall.at[1 - c, at_z(s)]
        return pltpu.make_async_remote_copy(
            ref, ref, ac_send.at[s], ac_recv.at[s], device_id=pal, device_id_type=MESH
        )

    def acts_core():
        for s in range(1, NZ):
            ref = aall.at[c, at_z(NZ - s)]
            pltpu.make_async_remote_copy(
                ref, ref, az_send.at[s - 1], az_recv.at[s - 1], device_id=dev_z(s), device_id_type=MESH
            ).wait_recv()
            to_pal(NZ - s).start()

    def partial(k, lo, hi):
        @pl.loop(lo, hi)
        def _(t):
            cols = pl.ds(pl.multiple_of(t * TILE, TILE), TILE)
            rows = pl.ds(pl.multiple_of(k * nk + t * TILE, TILE), TILE)
            both = lhs[:, k : k + 4].reshape(8 * half, lhs.shape[3])
            r = lax.dot_general(both, w[rows], (((1,), (1,)), ((), ())), preferred_element_type=F32)
            part[:, k, :, :, cols] = r.reshape(2, 4, half, TILE)

    def pair_copy(k):
        return pltpu.make_async_remote_copy(
            part.at[1 - c, k], pair.at[k], pr_send.at[k], pr_recv.at[k], device_id=pal, device_id_type=MESH
        )

    def scatter(k):
        pair_copy(k).wait_recv()
        part[c, k] += pair[k]
        todo = (((0, 2, mid.at[0]), (2, 1, near.at[0, 0]), (3, NZ - 1, near.at[1, 0])) if k == 0 else
                ((3, NZ - 2, mid.at[1]), (1, 1, near.at[0, 1]), (2, NZ - 1, near.at[1, 1])))
        out = []
        for i, (d, s, dst) in enumerate(todo):
            cp = pltpu.make_async_remote_copy(
                part.at[c, k, d], dst, rs_send.at[k * 3 + i], rs_recv.at[k * 3 + i],
                device_id=dev_z(s), device_id_type=MESH,
            )
            cp.start()
            out.append(cp)
        return out

    def fill():

        pb[0][0].from_far()
        pb[1][0].from_far()
        for d, s in enumerate((2, 0, 1, NZ - 1, NZ - 2)):
            to = at_z(s)
            lhs[0, d] = gp[to // NL, x, to % NL]
            lhs[1, d] = gq[to // NL, to % NL, x]
        own_w.wait()


    pa[0].own()
    qa[0].own()
    pb[0][0].own()
    qb[0][0].own()
    pa[0].from_left()
    pb[0][1].own()
    qa[0].from_left()
    qb[0][1].own()
    pa[0].from_right()
    qa[0].from_right()
    lr(pb[0][0])
    lr(qb[0][0])
    qb[0][2].own()
    hx_q.wait_recv()
    qa[1].own()
    qb[1][0].own()
    hx_p.wait_recv()
    pb[1][0].own()
    pa[1].own()
    acts_z()
    lr(qb[0][1])
    pa[0].from_far()
    lr(qa[1])
    lr(pb[1][0])
    pb[0][2].own()
    lr(pb[0][1])
    qa[0].from_far()
    qb[0][3].own()
    pb[0][3].own()
    qb[1][1].own()
    qb[1][2].own()
    lr(qb[0][2])
    qa[1].from_far()
    fill()
    qb[1][3].own()
    partial(0, 0, nk // TILE)
    pair_copy(0).start()
    grow(pa[1], pb[1])
    partial(1, 0, nk // TILE // 2)
    rs = scatter(0)
    partial(1, nk // TILE // 2, nk // TILE)
    pair_copy(1).start()
    lr(qb[1][0])
    lr(pb[0][2])
    pa[1].from_far()
    pb[1][3].own()
    rs += scatter(1)
    lr(pb[0][3])
    lr(qb[0][3])
    acts_core()
    for s in range(NZ):
        from_pal(s).wait_recv()
    for i in range(4):
        if i:
            pb[0][i].from_far()
        qb[0][i].from_far()
        group(True, h, xs[i])
        group(False, h, ys[i])
        if i < 3:
            lr(pb[1][1 + i])
            lr(qb[1][1 + i])
    for i in range(4):
        if i:
            pb[1][i].from_far()
        group(True, oh, xs[i])
        qb[1][i].from_far()
        group(False, oh, ys[i])

    for cp in rs:
        cp.wait_recv()
    gi_ref[:, :nk] = (part[c, 0, 1] + mid[0] + near[0, 0] + near[1, 0]).astype(BF16)
    gi_ref[:, nk:] = (part[c, 1, 0] + mid[1] + near[0, 1] + near[1, 1]).astype(BF16)
    gw_ref[0] = acc[...].astype(BF16)

    for r in pa + qa + pb[0] + pb[1] + qb[0] + qb[1]:
        r.wait_sent()
    for cp in sent + az + rs:
        cp.wait_send()
    for s in range(NZ):
        to_pal(s).wait_send()
    pair_copy(0).wait_send()
    pair_copy(1).wait_send()


def shards(acts, grad_out, weight):
    frames, width = acts.shape
    rows, hidden = grad_out.shape
    half = rows // 2
    kb = width // NZ
    nk = width // 2
    dma = pltpu.SemaphoreType.DMA
    return pl.pallas_call(
        kernel,
        out_shape=(
            jax.ShapeDtypeStruct((frames, width), BF16),
            jax.ShapeDtypeStruct((1, kb, hidden), BF16),
        ),
        in_specs=[pl.BlockSpec(memory_space=pl.ANY)] * 3,
        out_specs=(pl.BlockSpec(memory_space=pltpu.VMEM),) * 2,
        scratch_shapes=[
            pltpu.VMEM((NH, NX, NY, half, hidden), BF16),
            pltpu.VMEM((NH, NY, NX, half, hidden), BF16),
            pltpu.VMEM((width, hidden), BF16),
            pltpu.VMEM((frames, width), BF16),
            pltpu.VMEM((NH, NX, frames, kb), BF16),
            pltpu.VMEM((2, NZ, NX, frames, kb), BF16),
            pltpu.VMEM((kb, hidden), F32),
            pltpu.VMEM((2, 5, half, hidden), BF16),
            pltpu.VMEM((2, 2, 4, half, nk), F32),
            pltpu.VMEM((2, 4, half, nk), F32),
            pltpu.VMEM((2, 2, half, nk), F32),
            pltpu.VMEM((2, half, nk), F32),
            dma((80,)), dma((80,)), dma((4,)), dma((2,)), dma((2,)), dma((6,)), dma((6,)),
            dma((7,)), dma((7,)), dma((8,)), dma((8,)), dma((2,)), dma((2,)), dma((6,)), dma((6,)),
        ],
        compiler_params=pltpu.CompilerParams(
            collective_id=0, has_side_effects=True, vmem_limit_bytes=62 << 20
        ),
        name="grads",
    )(acts, grad_out, weight)


def solution(mesh):
    in_specs = (P(("dp", "col"), "row"), P(("dp", "row"), "col"), P("row", "col"))
    out_specs = (P(("dp", "col"), "row"), P("row", "dp", "col"))
    return jax.shard_map(shards, mesh=mesh, in_specs=in_specs, out_specs=out_specs, check_vma=False)
```

```python
import functools

import jax
import jax.numpy as jnp
from jax import lax
from jax.experimental import pallas as pl
from jax.experimental.pallas import tpu as pltpu
from jax.sharding import PartitionSpec as P

MESH = pl.DeviceIdType.MESH
F32 = jnp.float32
BF16 = jnp.bfloat16
NX = NY = NL = 4
NH = 2
NZ = NH * NL
TILE = 512


class Ring:
    def __init__(self, slot, loc, me, n, dev, send_sem, recv_sem):
        self.slot, self.loc, self.dev = slot, loc, dev
        self.me = me
        self.left, self.right, self.far = (lax.rem(me + s, n) for s in (n - 1, 1, 2))
        self.sends, self.recvs = send_sem, recv_sem

    def _copy(self, ref, k, to):
        i = self.slot * 4 + k
        return pltpu.make_async_remote_copy(
            ref, ref, self.sends.at[i], self.recvs.at[i], device_id=self.dev(to), device_id_type=MESH
        )

    def _half(self, o, k):
        ref = self.loc(o)
        rows = ref.shape[0] // 2
        return ref.at[pl.ds(k * rows, rows)]

    def own(self):
        self._copy(self.loc(self.me), 0, self.right).start()
        self._copy(self.loc(self.me), 1, self.left).start()

    def from_left(self):
        self._copy(self.loc(self.left), 0, self.right).wait_recv()
        self._copy(self._half(self.left, 0), 2, self.right).start()

    def from_right(self):
        self._copy(self.loc(self.right), 1, self.left).wait_recv()
        self._copy(self._half(self.right, 1), 3, self.left).start()

    def from_far(self):
        self._copy(self._half(self.far, 0), 2, self.right).wait_recv()
        self._copy(self._half(self.far, 1), 3, self.left).wait_recv()

    def wait_sent(self):
        self._copy(self.loc(self.me), 0, self.right).wait_send()
        self._copy(self.loc(self.me), 1, self.left).wait_send()
        self._copy(self._half(self.left, 0), 2, self.right).wait_send()
        self._copy(self._half(self.right, 1), 3, self.left).wait_send()


def kernel(
    acts_hbm, grad_hbm, w_hbm, gi_ref, gw_ref,
    gp, gq, w, acts, xbuf, aall, acc, lhs, part, pair, near, mid,
    ring_send, ring_recv, loc_sem, hx_send, hx_recv, ax_send, ax_recv, az_send, az_recv,
    ac_send, ac_recv, pr_send, pr_recv, rs_send, rs_recv,
):
    dp, y, col = lax.axis_index("dp"), lax.axis_index("row"), lax.axis_index("col")
    h, x, l, c = dp // NX, dp % NX, col // 2, col % 2
    z = h * NL + l
    oh = 1 - h
    half = gp.shape[3]
    kb = acts.shape[1] // NZ
    nk = part.shape[4]

    def dev_x(to):
        return (h * NX + to, y, col)

    def dev_y(to):
        return (dp, to, col)

    def at_z(s):
        return lax.rem(z + s, NZ)

    def dev_z(s):
        to = at_z(s)
        return ((to // NL) * NX + x, y, (to % NL) * 2 + c)

    pal = (dp, y, l * 2 + 1 - c)

    own_p = pltpu.make_async_copy(grad_hbm.at[pl.ds(0, half)], gp.at[h, x, y], loc_sem.at[0])
    own_q = pltpu.make_async_copy(grad_hbm.at[pl.ds(half, half)], gq.at[h, y, x], loc_sem.at[1])
    own_a = pltpu.make_async_copy(acts_hbm, acts, loc_sem.at[2])
    own_w = pltpu.make_async_copy(w_hbm, w, loc_sem.at[3])
    own_a.start()
    own_p.start()
    own_q.start()
    own_w.start()

    barrier = pltpu.get_barrier_semaphore()
    peers = [dev_x(lax.rem(x + s, NX)) for s in range(1, NX)]
    peers += [dev_y(lax.rem(y + s, NY)) for s in (1, NY - 1)]
    peers += [dev_z(s) for s in range(1, NZ)] + [pal]
    for peer in peers:
        pl.semaphore_signal(barrier, inc=1, device_id=peer, device_id_type=MESH)
    own_a.wait()
    own_p.wait()
    own_q.wait()
    pl.semaphore_wait(barrier, len(peers))

    sent = []

    hx_p = pltpu.make_async_remote_copy(
        gp.at[h, x, y], gp.at[h, x, y], hx_send.at[0], hx_recv.at[0], device_id=dev_z(NL), device_id_type=MESH
    )
    hx_q = pltpu.make_async_remote_copy(
        gq.at[h, y, x], gq.at[h, y, x], hx_send.at[1], hx_recv.at[1], device_id=dev_z(NL), device_id_type=MESH
    )
    ax = []
    for s in range(1, NX):
        to = lax.rem(x + s, NX)
        for b in range(NH):
            i = (s - 1) * NH + b
            cols = pl.ds(pl.multiple_of((b * NX + to) * kb, kb), kb)
            cp = pltpu.make_async_remote_copy(
                acts.at[:, cols], xbuf.at[b, x], ax_send.at[i], ax_recv.at[i],
                device_id=dev_x(to), device_id_type=MESH,
            )
            cp.start()
            ax.append(cp)
    hx_p.start()
    hx_q.start()
    sent += ax + [hx_p, hx_q]
    for b in range(NH):
        cols = pl.ds(pl.multiple_of((b * NX + x) * kb, kb), kb)
        xbuf[b, x] = acts[:, cols]

    slot = iter(range(20))

    def ring(axis, loc):
        me, dev = (x, dev_x) if axis == "x" else (y, dev_y)
        return Ring(next(slot), loc, me, NX, dev, ring_send, ring_recv)

    def p1(b):
        return ring("x", lambda o: gp.at[b, o, y])

    def p2(b, i):
        return ring("y", lambda o: gp.at[b, i, o])

    def q1(b):
        return ring("y", lambda o: gq.at[b, o, x])

    def q2(b, i):
        return ring("x", lambda o: gq.at[b, i, o])

    xs = [x, lax.rem(x + NX - 1, NX), lax.rem(x + 1, NX), lax.rem(x + 2, NX)]
    ys = [y, lax.rem(y + NY - 1, NY), lax.rem(y + 1, NY), lax.rem(y + 2, NY)]
    pa, qa = [p1(h), p1(oh)], [q1(h), q1(oh)]
    pb = [[p2(b, i) for i in xs] for b in (h, oh)]
    qb = [[q2(b, i) for i in ys] for b in (h, oh)]

    acc[...] = jnp.zeros_like(acc)
    wide = acc.shape[1] // 2

    def group(is_p, b, i):
        if is_p:
            a = jnp.concatenate([aall[0, b * NL + j, i] for j in range(NY)], axis=0)
            g = gp.at[b, i]
        else:
            a = aall[1, b * NL + i].reshape(NX * half, kb)
            g = gq.at[b, i]

        @pl.loop(0, acc.shape[1] // wide)
        def _(t):
            n = pl.ds(pl.multiple_of(t * wide, 128), wide)
            acc[:, n] += lax.dot_general(
                a, g[:, :, n].reshape(NX * half, wide), (((0,), (0,)), ((), ())), preferred_element_type=F32
            )

    az = []

    def acts_z():
        for cp in ax:
            cp.wait_recv()
        for s in (1, NZ - 1, 2, NZ - 2, 3, NZ - 3, 4):
            b = at_z(s) // NL
            cp = pltpu.make_async_remote_copy(
                xbuf.at[b], aall.at[c, z], az_send.at[s - 1], az_recv.at[s - 1],
                device_id=dev_z(s), device_id_type=MESH,
            )
            cp.start()
            az.append(cp)
        aall[c, z] = xbuf[h]
        to_pal(0).start()

    def to_pal(s):
        ref = aall.at[c, at_z(s)]
        return pltpu.make_async_remote_copy(
            ref, ref, ac_send.at[s], ac_recv.at[s], device_id=pal, device_id_type=MESH
        )

    def from_pal(s):
        ref = aall.at[1 - c, at_z(s)]
        return pltpu.make_async_remote_copy(
            ref, ref, ac_send.at[s], ac_recv.at[s], device_id=pal, device_id_type=MESH
        )

    def acts_core():
        for s in range(1, NZ):
            ref = aall.at[c, at_z(NZ - s)]
            pltpu.make_async_remote_copy(
                ref, ref, az_send.at[s - 1], az_recv.at[s - 1], device_id=dev_z(s), device_id_type=MESH
            ).wait_recv()
            to_pal(NZ - s).start()

    def partial(k, lo, hi):
        @pl.loop(lo, hi)
        def _(t):
            cols = pl.ds(pl.multiple_of(t * TILE, TILE), TILE)
            rows = pl.ds(pl.multiple_of(k * nk + t * TILE, TILE), TILE)
            both = lhs[:, k : k + 4].reshape(8 * half, lhs.shape[3])
            r = lax.dot_general(both, w[rows], (((1,), (1,)), ((), ())), preferred_element_type=F32)
            part[:, k, :, :, cols] = r.reshape(2, 4, half, TILE)

    def pair_copy(k):
        return pltpu.make_async_remote_copy(
            part.at[1 - c, k], pair.at[k], pr_send.at[k], pr_recv.at[k], device_id=pal, device_id_type=MESH
        )

    def scatter(k):
        pair_copy(k).wait_recv()
        part[c, k] += pair[k]
        todo = (((0, 2, mid.at[0]), (2, 1, near.at[0, 0]), (3, NZ - 1, near.at[1, 0])) if k == 0 else
                ((3, NZ - 2, mid.at[1]), (1, 1, near.at[0, 1]), (2, NZ - 1, near.at[1, 1])))
        out = []
        for i, (d, s, dst) in enumerate(todo):
            cp = pltpu.make_async_remote_copy(
                part.at[c, k, d], dst, rs_send.at[k * 3 + i], rs_recv.at[k * 3 + i],
                device_id=dev_z(s), device_id_type=MESH,
            )
            cp.start()
            out.append(cp)
        return out

    def fill():
        for d, s in enumerate((2, 0, 1, NZ - 1, NZ - 2)):
            to = at_z(s)
            lhs[0, d] = gp[to // NL, x, to % NL]
            lhs[1, d] = gq[to // NL, to % NL, x]
        own_w.wait()

    rs = []
    pb[0][0].own()
    pa[0].own()
    qb[0][0].own()
    qa[0].own()
    pa[0].from_right()
    pa[0].from_left()
    pb[0][2].own()
    qa[0].from_right()
    qb[0][2].own()
    pb[0][1].own()
    qa[0].from_left()
    hx_p.wait_recv()
    pb[1][0].own()
    pb[0][0].from_left()
    pa[1].own()
    pb[0][2].from_left()
    qb[0][1].own()
    qb[0][2].from_right()
    pb[0][1].from_right()
    qa[0].from_far()
    qb[0][3].own()
    acts_z()
    qb[0][2].from_left()
    pb[0][0].from_right()
    pa[1].from_right()
    hx_q.wait_recv()
    qb[0][1].from_left()
    qb[1][0].own()
    qa[1].own()
    pb[1][0].from_right()
    qb[0][0].from_right()
    pb[0][0].from_far()
    qb[0][1].from_right()
    qb[0][3].from_left()
    pb[1][0].from_left()
    pa[0].from_far()
    qb[0][3].from_right()
    pa[1].from_left()
    qa[1].from_left()
    qa[1].from_right()
    pb[1][1].own()
    qb[1][2].own()
    pb[0][2].from_right()
    pb[1][0].from_far()
    qb[0][0].from_left()
    pb[1][2].own()
    pb[0][3].own()
    qa[1].from_far()
    fill()
    qb[1][0].from_left()
    partial(1, 0, nk // TILE)
    pair_copy(1).start()
    qb[1][0].from_right()
    qb[1][3].own()
    rs += scatter(1)
    qb[0][3].from_far()
    qb[0][2].from_far()
    partial(0, 0, nk // TILE)
    pair_copy(0).start()
    acts_core()
    pb[0][1].from_left()
    qb[1][1].own()
    pb[1][2].from_right()
    pa[1].from_far()
    pb[1][3].own()
    pb[1][2].from_left()
    for s in range(NZ):
        from_pal(s).wait_recv()
    qb[1][0].from_far()
    group(True, h, xs[0])
    pb[0][3].from_right()
    qb[0][0].from_far()
    pb[0][2].from_far()
    qb[0][1].from_far()
    qb[1][2].from_left()
    group(True, oh, xs[0])
    rs += scatter(0)
    group(False, h, ys[2])
    pb[0][3].from_left()
    qb[1][2].from_right()
    group(False, h, ys[1])
    pb[0][1].from_far()
    group(False, oh, ys[0])
    pb[1][1].from_right()
    qb[1][3].from_right()
    group(False, h, ys[0])
    pb[1][1].from_left()
    pb[1][3].from_left()
    qb[1][3].from_left()
    group(False, h, ys[3])
    group(True, h, xs[2])
    qb[1][1].from_left()
    pb[1][3].from_right()
    qb[1][1].from_right()
    pb[1][2].from_far()
    pb[0][3].from_far()
    group(True, h, xs[3])
    qb[1][2].from_far()
    group(True, oh, xs[2])
    group(False, oh, ys[2])
    group(True, h, xs[1])
    qb[1][3].from_far()
    group(False, oh, ys[3])
    pb[1][1].from_far()
    group(True, oh, xs[1])
    pb[1][3].from_far()
    group(True, oh, xs[3])
    qb[1][1].from_far()
    group(False, oh, ys[1])

    for cp in rs:
        cp.wait_recv()
    gi_ref[:, :nk] = (part[c, 0, 1] + mid[0] + near[0, 0] + near[1, 0]).astype(BF16)
    gi_ref[:, nk:] = (part[c, 1, 0] + mid[1] + near[0, 1] + near[1, 1]).astype(BF16)
    gw_ref[0] = acc[...].astype(BF16)

    for r in pa + qa + pb[0] + pb[1] + qb[0] + qb[1]:
        r.wait_sent()
    for cp in sent + az + rs:
        cp.wait_send()
    for s in range(NZ):
        to_pal(s).wait_send()
    pair_copy(0).wait_send()
    pair_copy(1).wait_send()


def finish(gi_in, gw_in, gi_out, gw_out, gi_buf, gw_buf, sems):
    pairs = ((gw_in, gw_buf, gw_out), (gi_in, gi_buf, gi_out))
    into = [pltpu.make_async_copy(a, b, sems.at[k, 0]) for k, (a, b, _) in enumerate(pairs)]
    outof = [pltpu.make_async_copy(b, o, sems.at[k, 1]) for k, (_, b, o) in enumerate(pairs)]
    for cp in into:
        cp.start()
    for cp, out in zip(into, outof):
        cp.wait()
        out.start()
    for out in outof:
        out.wait()


def shards(acts, grad_out, weight):
    frames, width = acts.shape
    rows, hidden = grad_out.shape
    half = rows // 2
    kb = width // NZ
    nk = width // 2
    dma = pltpu.SemaphoreType.DMA
    gi, gw = pl.pallas_call(
        kernel,
        out_shape=(
            jax.ShapeDtypeStruct((frames, width), BF16),
            jax.ShapeDtypeStruct((1, kb, hidden), BF16),
        ),
        in_specs=[pl.BlockSpec(memory_space=pl.ANY)] * 3,
        out_specs=(pl.BlockSpec(memory_space=pltpu.VMEM),) * 2,
        scratch_shapes=[
            pltpu.VMEM((NH, NX, NY, half, hidden), BF16),
            pltpu.VMEM((NH, NY, NX, half, hidden), BF16),
            pltpu.VMEM((width, hidden), BF16),
            pltpu.VMEM((frames, width), BF16),
            pltpu.VMEM((NH, NX, frames, kb), BF16),
            pltpu.VMEM((2, NZ, NX, frames, kb), BF16),
            pltpu.VMEM((kb, hidden), F32),
            pltpu.VMEM((2, 5, half, hidden), BF16),
            pltpu.VMEM((2, 2, 4, half, nk), F32),
            pltpu.VMEM((2, 4, half, nk), F32),
            pltpu.VMEM((2, 2, half, nk), F32),
            pltpu.VMEM((2, half, nk), F32),
            dma((80,)), dma((80,)), dma((4,)), dma((2,)), dma((2,)), dma((6,)), dma((6,)),
            dma((7,)), dma((7,)), dma((8,)), dma((8,)), dma((2,)), dma((2,)), dma((6,)), dma((6,)),
        ],
        compiler_params=pltpu.CompilerParams(
            collective_id=0, has_side_effects=True, vmem_limit_bytes=62 << 20
        ),
        name="grads",
    )(acts, grad_out, weight)
    return pl.pallas_call(
        finish,
        out_shape=(jax.ShapeDtypeStruct(gi.shape, BF16), jax.ShapeDtypeStruct(gw.shape, BF16)),
        in_specs=[pl.BlockSpec(memory_space=pl.ANY)] * 2,
        out_specs=(pl.BlockSpec(memory_space=pl.ANY),) * 2,
        scratch_shapes=[pltpu.VMEM(gi.shape, BF16), pltpu.VMEM(gw.shape, BF16), dma((2, 2))],
        name="finish",
    )(gi, gw)


def solution(mesh):
    in_specs = (P(("dp", "col"), "row"), P(("dp", "row"), "col"), P("row", "col"))
    out_specs = (P(("dp", "col"), "row"), P("row", "dp", "col"))
    return jax.shard_map(shards, mesh=mesh, in_specs=in_specs, out_specs=out_specs, check_vma=False)
```

```python
import functools

import jax
import jax.numpy as jnp
from jax import lax
from jax.experimental import pallas as pl
from jax.experimental.pallas import tpu as pltpu
from jax.sharding import PartitionSpec as P

MESH = pl.DeviceIdType.MESH
F32 = jnp.float32
BF16 = jnp.bfloat16
NX = NY = NL = 4
NH = 2
NZ = NH * NL
TILE = 512


def chunks_of(hidden):
    return [(a * hidden // 14, n * hidden // 14) for a, n in ((0, 3), (3, 4), (7, 4), (11, 3))]


class Ring:
    def __init__(self, slot, loc, me, n, dev, send_sem, recv_sem):
        self.slot, self.loc, self.dev = slot, loc, dev
        self.me = me
        self.left, self.right, self.far = (lax.rem(me + s, n) for s in (n - 1, 1, 2))
        self.sends, self.recvs = send_sem, recv_sem

    def _copy(self, ref, k, to):
        i = self.slot * 4 + k
        return pltpu.make_async_remote_copy(
            ref, ref, self.sends.at[i], self.recvs.at[i], device_id=self.dev(to), device_id_type=MESH
        )

    def _half(self, o, k):
        ref = self.loc(o)
        rows = ref.shape[0] // 2
        return ref.at[pl.ds(k * rows, rows)]

    def own(self):
        self._copy(self.loc(self.me), 0, self.right).start()
        self._copy(self.loc(self.me), 1, self.left).start()

    def from_left(self):
        self._copy(self.loc(self.left), 0, self.right).wait_recv()
        self._copy(self._half(self.left, 0), 2, self.right).start()

    def from_right(self):
        self._copy(self.loc(self.right), 1, self.left).wait_recv()
        self._copy(self._half(self.right, 1), 3, self.left).start()

    def from_far(self):
        self._copy(self._half(self.far, 0), 2, self.right).wait_recv()
        self._copy(self._half(self.far, 1), 3, self.left).wait_recv()

    def wait_sent(self):
        self._copy(self.loc(self.me), 0, self.right).wait_send()
        self._copy(self.loc(self.me), 1, self.left).wait_send()
        self._copy(self._half(self.left, 0), 2, self.right).wait_send()
        self._copy(self._half(self.right, 1), 3, self.left).wait_send()


def kernel(
    acts_hbm, grad_hbm, w_hbm, gi_ref, gw_ref,
    gp, gq, w, acts, xbuf, aall, acc, wsend, wrecv, lhs, part, pair, near, mid,
    ring_send, ring_recv, pa_send, pa_recv, loc_sem, hx_send, hx_recv, ax_send, ax_recv, az_send, az_recv,
    ac_send, ac_recv, pr_send, pr_recv, rs_send, rs_recv, ws_send, ws_recv,
):
    dp, y, col = lax.axis_index("dp"), lax.axis_index("row"), lax.axis_index("col")
    h, x, l, c = dp // NX, dp % NX, col // 2, col % 2
    z = h * NL + l
    odd = x % 2
    px = x + 1 - 2 * odd
    bx = (x + 2 * odd + NX - 1) % NX
    pbx = (px + 2 - 2 * odd + NX - 1) % NX
    half = gp.shape[3]
    kb = acts.shape[1] // NZ
    nk = part.shape[4]
    cuts = chunks_of(gp.shape[4])
    nj = len(cuts)

    def dev_x(to):
        return (h * NX + to, y, col)

    def dev_y(to):
        return (dp, to, col)

    def at_z(s):
        return lax.rem(z + s, NZ)

    def dev_z(s):
        to = at_z(s)
        return ((to // NL) * NX + x, y, (to % NL) * 2 + c)

    def side(to):
        return (to // NL + h) % 2

    pal = (dp, y, l * 2 + 1 - c)

    own_p = pltpu.make_async_copy(grad_hbm.at[pl.ds(0, half)], gp.at[0, 0, y], loc_sem.at[0])
    own_q = pltpu.make_async_copy(grad_hbm.at[pl.ds(half, half)], gq.at[0, 0, y], loc_sem.at[1])
    own_a = pltpu.make_async_copy(acts_hbm, acts, loc_sem.at[2])
    own_w = pltpu.make_async_copy(w_hbm, w, loc_sem.at[3])
    own_a.start()
    own_p.start()
    own_q.start()
    own_w.start()

    barrier = pltpu.get_barrier_semaphore()
    peers = [dev_x(px), dev_x(bx)] + [dev_y(lax.rem(y + s, NY)) for s in (1, NY - 1)]
    peers += [dev_z(s) for s in range(1, NZ)] + [pal]
    for peer in peers:
        pl.semaphore_signal(barrier, inc=1, device_id=peer, device_id_type=MESH)
    own_a.wait()
    own_p.wait()
    own_q.wait()
    pl.semaphore_wait(barrier, len(peers))

    def remote(src, dst, send, recv, i, to):
        return pltpu.make_async_remote_copy(
            src, dst, send.at[i], recv.at[i], device_id=to, device_id_type=MESH
        )

    def lanes(j):
        return pl.ds(cuts[j][0], cuts[j][1])

    class Chunk:
        def __init__(self, b, j):
            self.b, self.j, self.i = b, j, b * nj + j
            n = lanes(j)

            def ring(k, ref, s):
                return Ring(
                    k * NH * nj + self.i, lambda o: ref.at[b, s, o, :, n], y, NY, dev_y, ring_send, ring_recv
                )

            self.yq, self.y0, self.y1 = ring(0, gq, 0), ring(1, gp, 0), ring(2, gp, 1)
            self.pa = remote(
                gp.at[b, 0, y, :, n], gp.at[b, 1, y, :, n], pa_send, pa_recv, self.i * 5 + 4, dev_x(px)
            )
            self.qa = [
                remote(gq.at[b, 0, o, :, n], gq.at[b, 1, o, :, n], pa_send, pa_recv, self.i * 5 + k, dev_x(px))
                for k, o in enumerate(lax.rem(y + s, NY) for s in (0, NY - 1, 1, 2))
            ]
            self.hx = [
                remote(ref.at[0, 0, y, :, n], ref.at[1, 0, y, :, n], hx_send, hx_recv, j * 2 + k, dev_z(NL))
                for k, ref in enumerate((gp, gq))
            ]

        def byq(self):
            if self.b:
                self.hx[1].wait_recv()
            self.yq.own()

        def by0(self):
            if self.b:
                self.hx[0].wait_recv()
            self.y0.own()

        def bpa(self):
            self.pa.start()

        def bqa(self):
            self.qa[0].start()

        def mql(self):
            self.yq.from_left()
            self.qa[1].start()

        def mqr(self):
            self.yq.from_right()
            self.qa[2].start()

        def m0(self):
            self.y0.from_left()
            self.y0.from_right()

        def mp(self):
            self.pa.wait_recv()
            self.y1.own()

        def eq(self):
            self.yq.from_far()
            self.qa[3].start()

        def ep(self):
            self.y1.from_left()
            self.y1.from_right()

        def e0(self):
            self.y0.from_far()

        def dn(self):
            self.y1.from_far()
            for q in self.qa:
                q.wait_recv()

        def wait_sent(self):
            for r in (self.yq, self.y0, self.y1):
                r.wait_sent()
            for cp in self.qa + [self.pa]:
                cp.wait_send()
            if not self.b:
                for cp in self.hx:
                    cp.wait_send()

    ch = [[Chunk(b, j) for j in range(nj)] for b in range(NH)]

    ax = []
    for b in range(NH):
        for r, (theirs, mine) in enumerate(((pbx, bx), (px, x))):
            cols = pl.ds(pl.multiple_of((b * NX + theirs) * kb, kb), kb)
            ax.append(remote(acts.at[:, cols], xbuf.at[b, r, 1], ax_send, ax_recv, b * 2 + r, dev_x(px)))
            ax[-1].start()
            cols = pl.ds(pl.multiple_of((b * NX + mine) * kb, kb), kb)
            xbuf[b, r, 0] = acts[:, cols]

    def az(r, s, to):
        b = at_z(s) // NL
        return remote(
            xbuf.at[b, r], aall.at[r, c, side(to), :, to % NL], az_send, az_recv, r * NZ + s, dev_z(s)
        )

    def acts_z(r):
        for s in (1, NZ - 1, 2, NZ - 2, 3, NZ - 3, 4):
            b = at_z(s) // NL
            remote(
                xbuf.at[b, r], aall.at[r, c, (b + h) % 2, :, l], az_send, az_recv, r * NZ + s, dev_z(s)
            ).start()
        aall[r, c, 0, :, l] = xbuf[h, r]

    def ac(r, cc):
        return remote(aall.at[r, cc], aall.at[r, cc], ac_send, ac_recv, r, pal)

    def acts_core(r):
        for s in range(1, NZ):
            az(r, s, at_z(NZ - s)).wait_recv()
        ac(r, c).start()

    def wgrad(r, j):
        n = lanes(j)
        out = None
        for cc, g in enumerate((gp, gq)):
            t = lax.dot_general(
                aall[r, cc].reshape(-1, kb), g[:, :, :, :, n].reshape(-1, cuts[j][1]),
                (((0,), (0,)), ((), ())), preferred_element_type=F32,
            )
            out = t if out is None else out + t
        if r:
            acc[:, n] = out
        else:
            wsend[:, n] = out

    def ws(j):
        return remote(wsend.at[:, lanes(j)], wrecv.at[:, lanes(j)], ws_send, ws_recv, j, dev_x(bx))

    def fill():
        for d, s in enumerate((2, 0, 1, NZ - 1, NZ - 2)):
            to = at_z(s)
            lhs[0, d] = gp[side(to), 0, to % NL]
            lhs[1, d] = gq[side(to), 0, to % NL]

    def partial(k, lo, hi):
        @pl.loop(lo, hi)
        def _(t):
            cols = pl.ds(pl.multiple_of(t * TILE, TILE), TILE)
            rows = pl.ds(pl.multiple_of(k * nk + t * TILE, TILE), TILE)
            both = lhs[:, k : k + 4].reshape(8 * half, lhs.shape[3])
            r = lax.dot_general(both, w[rows], (((1,), (1,)), ((), ())), preferred_element_type=F32)
            part[:, k, :, :, cols] = r.reshape(2, 4, half, TILE)

    def pair_copy(k):
        return remote(part.at[1 - c, k], pair.at[k], pr_send, pr_recv, k, pal)

    def scatter(k):
        pair_copy(k).wait_recv()
        part[c, k] += pair[k]
        todo = (((0, 2, mid.at[0]), (2, 1, near.at[0, 0]), (3, NZ - 1, near.at[1, 0])) if k == 0 else
                ((3, NZ - 2, mid.at[1]), (1, 1, near.at[0, 1]), (2, NZ - 1, near.at[1, 1])))
        out = []
        for i, (d, s, dst) in enumerate(todo):
            out.append(remote(part.at[c, k, d], dst, rs_send, rs_recv, k * 3 + i, dev_z(s)))
            out[-1].start()
        return out

    def hx(j):
        for cp in ch[0][j].hx:
            cp.start()

    rs = []
    hx(3)
    ch[0][3].by0()
    ch[0][2].byq()
    ch[0][0].byq()
    hx(2)
    ch[0][2].bqa()
    ch[0][2].by0()
    ch[0][3].byq()
    ch[0][1].byq()
    hx(0)
    ch[0][2].bpa()
    ch[0][0].bqa()
    for cp in ax:
        cp.wait_recv()
    ch[0][2].mql()
    ch[1][3].byq()
    ch[0][0].bpa()
    ch[0][1].bpa()
    ch[0][2].m0()
    ch[0][3].mqr()
    ch[0][0].by0()
    ch[0][2].mqr()
    ch[1][3].mqr()
    ch[1][3].by0()
    ch[1][3].bqa()
    ch[1][2].byq()
    ch[0][2].mp()
    ch[0][0].mql()
    ch[0][3].bpa()
    ch[1][3].bpa()
    ch[0][2].e0()
    ch[1][3].m0()
    ch[1][2].by0()
    ch[0][1].by0()
    ch[1][2].bpa()
    acts_z(0)
    ch[1][2].mql()
    ch[0][0].mqr()
    ch[0][2].ep()
    ch[1][2].bqa()
    ch[0][2].eq()
    ch[1][0].byq()
    ch[1][3].mql()
    ch[1][2].mqr()
    ch[1][0].by0()
    ch[1][2].m0()
    ch[1][0].mqr()
    ch[1][2].mp()
    ch[0][0].m0()
    ch[1][0].m0()
    ch[0][1].m0()
    ch[1][0].bpa()
    ch[1][2].eq()
    ch[0][1].mqr()
    ch[1][0].mql()
    hx(1)
    ch[1][2].ep()
    ch[0][3].mp()
    ch[0][0].mp()
    ch[0][3].mql()
    ch[0][1].mql()
    ch[1][2].e0()
    ch[0][0].e0()
    ch[0][1].mp()
    acts_core(0)
    ch[1][0].mp()
    ch[1][0].eq()
    ch[1][0].bqa()
    ch[0][3].m0()
    ch[0][3].ep()
    ch[0][0].eq()
    ch[1][2].dn()
    ch[0][0].ep()
    ch[1][3].mp()
    ch[0][3].eq()
    ch[1][3].e0()
    ac(0, 1 - c).wait_recv()
    ch[0][2].dn()
    ch[1][0].e0()
    wgrad(0, 2)
    ws(2).start()
    ch[1][0].ep()
    ch[1][1].byq()
    acts_z(1)
    ch[1][1].by0()
    ch[0][1].bqa()
    ch[0][1].eq()
    ch[1][1].mql()
    ch[0][0].dn()
    ch[1][1].bpa()
    ch[1][1].mqr()
    ch[0][3].e0()
    ch[1][1].m0()
    ch[1][0].dn()
    ch[1][3].ep()
    wgrad(0, 0)
    ws(0).start()
    ch[0][1].e0()
    ch[1][1].eq()
    ch[0][3].bqa()
    ch[1][1].bqa()
    ch[1][3].eq()
    ch[0][1].ep()
    ch[1][1].e0()
    own_w.wait()
    fill()
    partial(1, 0, nk // TILE)
    pair_copy(1).start()
    partial(0, 0, nk // TILE)
    pair_copy(0).start()
    rs += scatter(1)
    ch[1][3].dn()
    ch[1][1].mp()
    acts_core(1)
    ch[0][3].dn()
    wgrad(0, 3)
    ws(3).start()
    ch[0][1].dn()
    ch[1][1].ep()
    ch[1][1].dn()
    wgrad(0, 1)
    ws(1).start()
    rs += scatter(0)
    ac(1, 1 - c).wait_recv()
    wgrad(1, 1)
    wgrad(1, 3)
    wgrad(1, 0)
    wgrad(1, 2)

    for j in range(nj):
        ws(j).wait_recv()
        n = lanes(j)
        gw_ref[0, :, n] = (acc[:, n] + wrecv[:, n]).astype(BF16)
    for cp in rs:
        cp.wait_recv()
    gi_ref[:, :nk] = (part[c, 0, 1] + mid[0] + near[0, 0] + near[1, 0]).astype(BF16)
    gi_ref[:, nk:] = (part[c, 1, 0] + mid[1] + near[0, 1] + near[1, 1]).astype(BF16)

    for b in range(NH):
        for j in range(nj):
            ch[b][j].wait_sent()
    for r in range(2):
        for s in range(1, NZ):
            az(r, s, z).wait_send()
        ac(r, c).wait_send()
    for j in range(nj):
        ws(j).wait_send()
    for cp in ax + rs:
        cp.wait_send()
    pair_copy(0).wait_send()
    pair_copy(1).wait_send()


def finish(gi_in, gw_in, gi_out, gw_out, gi_buf, gw_buf, sems):
    pairs = ((gw_in, gw_buf, gw_out), (gi_in, gi_buf, gi_out))
    into = [pltpu.make_async_copy(a, b, sems.at[k, 0]) for k, (a, b, _) in enumerate(pairs)]
    outof = [pltpu.make_async_copy(b, o, sems.at[k, 1]) for k, (_, b, o) in enumerate(pairs)]
    for cp in into:
        cp.start()
    for cp, out in zip(into, outof):
        cp.wait()
        out.start()
    for out in outof:
        out.wait()


def shards(acts, grad_out, weight):
    frames, width = acts.shape
    rows, hidden = grad_out.shape
    half = rows // 2
    kb = width // NZ
    nk = width // 2
    nj = len(chunks_of(hidden))
    dma = pltpu.SemaphoreType.DMA
    counts = [3 * NH * nj * 4] * 2 + [5 * NH * nj] * 2 + [4] + [2 * nj] * 2 + [4] * 2 + [2 * NZ] * 2
    counts += [2] * 2 + [2] * 2 + [6] * 2 + [nj] * 2
    gi, gw = pl.pallas_call(
        kernel,
        out_shape=(
            jax.ShapeDtypeStruct((frames, width), BF16),
            jax.ShapeDtypeStruct((1, kb, hidden), BF16),
        ),
        in_specs=[pl.BlockSpec(memory_space=pl.ANY)] * 3,
        out_specs=(pl.BlockSpec(memory_space=pltpu.VMEM),) * 2,
        scratch_shapes=[
            pltpu.VMEM((NH, 2, NY, half, hidden), BF16),
            pltpu.VMEM((NH, 2, NY, half, hidden), BF16),
            pltpu.VMEM((width, hidden), BF16),
            pltpu.VMEM((frames, width), BF16),
            pltpu.VMEM((NH, 2, 2, frames, kb), BF16),
            pltpu.VMEM((2, 2, NH, 2, NL, frames, kb), BF16),
            pltpu.VMEM((kb, hidden), F32),
            pltpu.VMEM((kb, hidden), F32),
            pltpu.VMEM((kb, hidden), F32),
            pltpu.VMEM((2, 5, half, hidden), BF16),
            pltpu.VMEM((2, 2, 4, half, nk), F32),
            pltpu.VMEM((2, 4, half, nk), F32),
            pltpu.VMEM((2, 2, half, nk), F32),
            pltpu.VMEM((2, half, nk), F32),
        ]
        + [dma((n,)) for n in counts],
        compiler_params=pltpu.CompilerParams(
            collective_id=0, has_side_effects=True, vmem_limit_bytes=62 << 20
        ),
        name="grads",
    )(acts, grad_out, weight)
    return pl.pallas_call(
        finish,
        out_shape=(jax.ShapeDtypeStruct(gi.shape, BF16), jax.ShapeDtypeStruct(gw.shape, BF16)),
        in_specs=[pl.BlockSpec(memory_space=pl.ANY)] * 2,
        out_specs=(pl.BlockSpec(memory_space=pl.ANY),) * 2,
        scratch_shapes=[pltpu.VMEM(gi.shape, BF16), pltpu.VMEM(gw.shape, BF16), dma((2, 2))],
        name="finish",
    )(gi, gw)


def solution(mesh):
    in_specs = (P(("dp", "col"), "row"), P(("dp", "row"), "col"), P("row", "col"))
    out_specs = (P(("dp", "col"), "row"), P("row", "dp", "col"))
    return jax.shard_map(shards, mesh=mesh, in_specs=in_specs, out_specs=out_specs, check_vma=False)
```

```python
import functools

import jax
import jax.numpy as jnp
from jax import lax
from jax.experimental import pallas as pl
from jax.experimental.pallas import tpu as pltpu
from jax.sharding import PartitionSpec as P

MESH = pl.DeviceIdType.MESH
F32 = jnp.float32
BF16 = jnp.bfloat16
NX = NY = NL = 4
NH = 2
NZ = NH * NL
TILE = 512


def chunks_of(hidden):
    return [(a * hidden // 14, n * hidden // 14) for a, n in ((0, 3), (3, 4), (7, 4), (11, 3))]


class Ring:
    def __init__(self, slot, loc, me, n, dev, send_sem, recv_sem):
        self.slot, self.loc, self.dev = slot, loc, dev
        self.me = me
        self.left, self.right, self.far = (lax.rem(me + s, n) for s in (n - 1, 1, 2))
        self.sends, self.recvs = send_sem, recv_sem

    def _copy(self, ref, k, to):
        i = self.slot * 4 + k
        return pltpu.make_async_remote_copy(
            ref, ref, self.sends.at[i], self.recvs.at[i], device_id=self.dev(to), device_id_type=MESH
        )

    def _half(self, o, k):
        ref = self.loc(o)
        rows = ref.shape[0] // 2
        return ref.at[pl.ds(k * rows, rows)]

    def own(self):
        self._copy(self.loc(self.me), 0, self.right).start()
        self._copy(self.loc(self.me), 1, self.left).start()

    def from_left(self):
        self._copy(self.loc(self.left), 0, self.right).wait_recv()
        self._copy(self._half(self.left, 0), 2, self.right).start()

    def from_right(self):
        self._copy(self.loc(self.right), 1, self.left).wait_recv()
        self._copy(self._half(self.right, 1), 3, self.left).start()

    def from_far(self):
        self._copy(self._half(self.far, 0), 2, self.right).wait_recv()
        self._copy(self._half(self.far, 1), 3, self.left).wait_recv()

    def wait_sent(self):
        self._copy(self.loc(self.me), 0, self.right).wait_send()
        self._copy(self.loc(self.me), 1, self.left).wait_send()
        self._copy(self._half(self.left, 0), 2, self.right).wait_send()
        self._copy(self._half(self.right, 1), 3, self.left).wait_send()


def kernel(
    acts_hbm, grad_hbm, w_hbm, gi_ref, gw_ref,
    gp, gq, w, acts, xbuf, aall, acc, wsend, wrecv, lhs, part, pair, near, mid,
    ring_send, ring_recv, pa_send, pa_recv, loc_sem, hx_send, hx_recv, ax_send, ax_recv, az_send, az_recv,
    ac_send, ac_recv, pr_send, pr_recv, rs_send, rs_recv, ws_send, ws_recv,
):
    dp, y, col = lax.axis_index("dp"), lax.axis_index("row"), lax.axis_index("col")
    h, x, l, c = dp // NX, dp % NX, col // 2, col % 2
    z = h * NL + l
    odd = x % 2
    px = x + 1 - 2 * odd
    bx = (x + 2 * odd + NX - 1) % NX
    pbx = (px + 2 - 2 * odd + NX - 1) % NX
    half = gp.shape[3]
    kb = acts.shape[1] // NZ
    nk = part.shape[4]
    cuts = chunks_of(gp.shape[4])
    nj = len(cuts)

    def dev_x(to):
        return (h * NX + to, y, col)

    def dev_y(to):
        return (dp, to, col)

    def at_z(s):
        return lax.rem(z + s, NZ)

    def dev_z(s):
        to = at_z(s)
        return ((to // NL) * NX + x, y, (to % NL) * 2 + c)

    def side(to):
        return (to // NL + h) % 2

    pal = (dp, y, l * 2 + 1 - c)

    own_p = pltpu.make_async_copy(grad_hbm.at[pl.ds(0, half)], gp.at[0, 0, y], loc_sem.at[0])
    own_q = pltpu.make_async_copy(grad_hbm.at[pl.ds(half, half)], gq.at[0, 0, y], loc_sem.at[1])
    own_a = pltpu.make_async_copy(acts_hbm, acts, loc_sem.at[2])
    own_w = pltpu.make_async_copy(w_hbm, w, loc_sem.at[3])
    own_a.start()
    own_p.start()
    own_q.start()
    own_w.start()

    barrier = pltpu.get_barrier_semaphore()
    peers = [dev_x(px), dev_x(bx)] + [dev_y(lax.rem(y + s, NY)) for s in (1, NY - 1)]
    peers += [dev_z(s) for s in range(1, NZ)] + [pal]
    for peer in peers:
        pl.semaphore_signal(barrier, inc=1, device_id=peer, device_id_type=MESH)
    own_a.wait()
    own_p.wait()
    own_q.wait()
    pl.semaphore_wait(barrier, len(peers))

    def remote(src, dst, send, recv, i, to):
        return pltpu.make_async_remote_copy(
            src, dst, send.at[i], recv.at[i], device_id=to, device_id_type=MESH
        )

    def lanes(j):
        return pl.ds(cuts[j][0], cuts[j][1])

    class Chunk:
        def __init__(self, b, j):
            self.b, self.j, self.i = b, j, b * nj + j
            n = lanes(j)

            def ring(k, ref, s):
                return Ring(
                    k * NH * nj + self.i, lambda o: ref.at[b, s, o, :, n], y, NY, dev_y, ring_send, ring_recv
                )

            self.yq, self.y0, self.y1 = ring(0, gq, 0), ring(1, gp, 0), ring(2, gp, 1)
            self.pa = remote(
                gp.at[b, 0, y, :, n], gp.at[b, 1, y, :, n], pa_send, pa_recv, self.i * 5 + 4, dev_x(px)
            )
            self.qa = [
                remote(gq.at[b, 0, o, :, n], gq.at[b, 1, o, :, n], pa_send, pa_recv, self.i * 5 + k, dev_x(px))
                for k, o in enumerate(lax.rem(y + s, NY) for s in (0, NY - 1, 1, 2))
            ]
            self.hx = [
                remote(ref.at[0, 0, y, :, n], ref.at[1, 0, y, :, n], hx_send, hx_recv, j * 2 + k, dev_z(NL))
                for k, ref in enumerate((gp, gq))
            ]

        def byq(self):
            if self.b:
                self.hx[1].wait_recv()
            self.yq.own()

        def by0(self):
            if self.b:
                self.hx[0].wait_recv()
            self.y0.own()

        def bpa(self):
            self.pa.start()

        def bqa(self):
            self.qa[0].start()

        def mql(self):
            self.yq.from_left()
            self.qa[1].start()

        def mqr(self):
            self.yq.from_right()
            self.qa[2].start()

        def m0(self):
            self.y0.from_left()
            self.y0.from_right()

        def mp(self):
            self.pa.wait_recv()
            self.y1.own()

        def eq(self):
            self.yq.from_far()
            self.qa[3].start()

        def ep(self):
            self.y1.from_left()
            self.y1.from_right()

        def e0(self):
            self.y0.from_far()

        def dn(self):
            self.y1.from_far()
            for q in self.qa:
                q.wait_recv()

        def wait_sent(self):
            for r in (self.yq, self.y0, self.y1):
                r.wait_sent()
            for cp in self.qa + [self.pa]:
                cp.wait_send()
            if not self.b:
                for cp in self.hx:
                    cp.wait_send()

    ch = [[Chunk(b, j) for j in range(nj)] for b in range(NH)]

    ax = []
    for b in range(NH):
        for r, (theirs, mine) in enumerate(((pbx, bx), (px, x))):
            cols = pl.ds(pl.multiple_of((b * NX + theirs) * kb, kb), kb)
            ax.append(remote(acts.at[:, cols], xbuf.at[b, r, 1], ax_send, ax_recv, b * 2 + r, dev_x(px)))
            ax[-1].start()
            cols = pl.ds(pl.multiple_of((b * NX + mine) * kb, kb), kb)
            xbuf[b, r, 0] = acts[:, cols]

    def az(r, s, to):
        b = at_z(s) // NL
        return remote(
            xbuf.at[b, r], aall.at[r, c, side(to), :, to % NL], az_send, az_recv, r * NZ + s, dev_z(s)
        )

    def acts_z(r):
        for s in (1, NZ - 1, 2, NZ - 2, 3, NZ - 3, 4):
            b = at_z(s) // NL
            remote(
                xbuf.at[b, r], aall.at[r, c, (b + h) % 2, :, l], az_send, az_recv, r * NZ + s, dev_z(s)
            ).start()
        aall[r, c, 0, :, l] = xbuf[h, r]

    def ac(r, cc):
        return remote(aall.at[r, cc], aall.at[r, cc], ac_send, ac_recv, r, pal)

    def acts_core(r):
        for s in range(1, NZ):
            az(r, s, at_z(NZ - s)).wait_recv()
        ac(r, c).start()

    def wgrad(r, j):
        n = lanes(j)
        out = None
        for cc, g in enumerate((gp, gq)):
            t = lax.dot_general(
                aall[r, cc].reshape(-1, kb), g[:, :, :, :, n].reshape(-1, cuts[j][1]),
                (((0,), (0,)), ((), ())), preferred_element_type=F32,
            )
            out = t if out is None else out + t
        if r:
            acc[:, n] = out
        else:
            wsend[:, n] = out

    def ws(j):
        return remote(wsend.at[:, lanes(j)], wrecv.at[:, lanes(j)], ws_send, ws_recv, j, dev_x(bx))

    def fill():
        for d, s in enumerate((2, 0, 1, NZ - 1, NZ - 2)):
            to = at_z(s)
            lhs[0, d] = gp[side(to), 0, to % NL]
            lhs[1, d] = gq[side(to), 0, to % NL]

    def partial(k, lo, hi):
        @pl.loop(lo, hi)
        def _(t):
            cols = pl.ds(pl.multiple_of(t * TILE, TILE), TILE)
            rows = pl.ds(pl.multiple_of(k * nk + t * TILE, TILE), TILE)
            both = lhs[:, k : k + 4].reshape(8 * half, lhs.shape[3])
            r = lax.dot_general(both, w[rows], (((1,), (1,)), ((), ())), preferred_element_type=F32)
            part[:, k, :, :, cols] = r.reshape(2, 4, half, TILE)

    def pair_copy(k):
        return remote(part.at[1 - c, k], pair.at[k], pr_send, pr_recv, k, pal)

    def scatter(k):
        pair_copy(k).wait_recv()
        part[c, k] += pair[k]
        todo = (((0, 2, mid.at[0]), (2, 1, near.at[0, 0]), (3, NZ - 1, near.at[1, 0])) if k == 0 else
                ((3, NZ - 2, mid.at[1]), (1, 1, near.at[0, 1]), (2, NZ - 1, near.at[1, 1])))
        out = []
        for i, (d, s, dst) in enumerate(todo):
            out.append((k, remote(part.at[c, k, d], dst, rs_send, rs_recv, k * 3 + i, dev_z(s))))
            out[-1][1].start()
        return out

    def hx(j):
        for cp in ch[0][j].hx:
            cp.start()

    rs = []
    hx(3)
    ch[0][3].by0()
    ch[0][2].byq()
    ch[0][0].byq()
    hx(2)
    ch[0][2].bqa()
    ch[0][2].by0()
    ch[0][3].byq()
    ch[0][1].byq()
    hx(0)
    ch[0][2].bpa()
    ch[0][0].bqa()
    for cp in ax:
        cp.wait_recv()
    ch[0][2].mql()
    ch[1][3].byq()
    ch[0][0].bpa()
    ch[0][1].bpa()
    ch[0][2].m0()
    ch[0][3].mqr()
    ch[0][0].by0()
    ch[0][2].mqr()
    ch[1][3].mqr()
    ch[1][3].by0()
    ch[1][3].bqa()
    ch[1][2].byq()
    ch[0][2].mp()
    ch[0][0].mql()
    ch[0][3].bpa()
    ch[1][3].bpa()
    ch[0][2].e0()
    ch[1][3].m0()
    ch[1][2].by0()
    ch[0][1].by0()
    ch[1][2].bpa()
    acts_z(0)
    ch[1][2].mql()
    ch[0][0].mqr()
    ch[0][2].ep()
    ch[1][2].bqa()
    ch[0][2].eq()
    ch[1][0].byq()
    ch[1][3].mql()
    ch[1][2].mqr()
    ch[1][0].by0()
    ch[1][2].m0()
    ch[1][0].mqr()
    ch[1][2].mp()
    ch[0][0].m0()
    ch[1][0].m0()
    ch[0][1].m0()
    ch[1][0].bpa()
    ch[1][2].eq()
    ch[0][1].mqr()
    ch[1][0].mql()
    hx(1)
    ch[1][2].ep()
    ch[0][3].mp()
    ch[0][0].mp()
    ch[0][3].mql()
    ch[0][1].mql()
    ch[1][2].e0()
    ch[0][0].e0()
    ch[0][1].mp()
    acts_core(0)
    ch[1][0].mp()
    ch[1][0].eq()
    ch[1][0].bqa()
    ch[0][3].m0()
    ch[0][3].ep()
    ch[0][0].eq()
    ch[1][2].dn()
    ch[0][0].ep()
    ch[1][3].mp()
    ch[0][3].eq()
    ch[1][3].e0()
    ac(0, 1 - c).wait_recv()
    ch[0][2].dn()
    ch[1][0].e0()
    wgrad(0, 2)
    ws(2).start()
    ch[1][0].ep()
    ch[1][1].byq()
    acts_z(1)
    ch[1][1].by0()
    ch[0][1].bqa()
    ch[0][1].eq()
    ch[1][1].mql()
    ch[0][0].dn()
    ch[1][1].bpa()
    ch[1][1].mqr()
    ch[0][3].e0()
    ch[1][1].m0()
    ch[1][0].dn()
    ch[1][3].ep()
    wgrad(0, 0)
    ws(0).start()
    ch[0][1].e0()
    ch[1][1].eq()
    ch[0][3].bqa()
    ch[1][1].bqa()
    ch[1][3].eq()
    ch[0][1].ep()
    ch[1][1].e0()
    own_w.wait()
    fill()
    partial(1, 0, nk // TILE)
    pair_copy(1).start()
    partial(0, 0, nk // TILE)
    pair_copy(0).start()
    rs += scatter(1)
    ch[1][3].dn()
    ch[1][1].mp()
    acts_core(1)
    ch[0][3].dn()
    wgrad(0, 3)
    ws(3).start()
    ch[0][1].dn()
    ch[1][1].ep()
    ch[1][1].dn()
    wgrad(0, 1)
    ws(1).start()
    rs += scatter(0)
    ac(1, 1 - c).wait_recv()
    wgrad(1, 1)
    wgrad(1, 3)
    wgrad(1, 0)
    wgrad(1, 2)

    def gw_piece(j):
        ws(j).wait_recv()
        n = lanes(j)
        gw_ref[0, :, n] = (acc[:, n] + wrecv[:, n]).astype(BF16)

    def gi_piece(k):
        for cp in rs:
            if cp[0] == k:
                cp[1].wait_recv()
        cols = pl.ds(k * nk, nk)
        gi_ref[:, cols] = (part[c, k, 1 - k] + mid[k] + near[0, k] + near[1, k]).astype(BF16)

    for j in (2, 0):
        gw_piece(j)
    gi_piece(1)
    gw_piece(3)
    gi_piece(0)
    gw_piece(1)

    for b in range(NH):
        for j in range(nj):
            ch[b][j].wait_sent()
    for r in range(2):
        for s in range(1, NZ):
            az(r, s, z).wait_send()
        ac(r, c).wait_send()
    for j in range(nj):
        ws(j).wait_send()
    for cp in ax + [cp for _, cp in rs]:
        cp.wait_send()
    pair_copy(0).wait_send()
    pair_copy(1).wait_send()


def finish(gi_in, gw_in, gi_out, gw_out, sems):
    a = pltpu.make_async_copy(gi_in, gi_out, sems.at[0])
    b = pltpu.make_async_copy(gw_in, gw_out, sems.at[1])
    b.start()
    a.start()
    a.wait()
    b.wait()


def shards(acts, grad_out, weight):
    frames, width = acts.shape
    rows, hidden = grad_out.shape
    half = rows // 2
    kb = width // NZ
    nk = width // 2
    nj = len(chunks_of(hidden))
    dma = pltpu.SemaphoreType.DMA
    counts = [3 * NH * nj * 4] * 2 + [5 * NH * nj] * 2 + [4] + [2 * nj] * 2 + [4] * 2 + [2 * NZ] * 2
    counts += [2] * 2 + [2] * 2 + [6] * 2 + [nj] * 2
    gi, gw = pl.pallas_call(
        kernel,
        out_shape=(
            pltpu.VMEM((frames, width), BF16),
            pltpu.VMEM((1, kb, hidden), BF16),
        ),
        in_specs=[pl.BlockSpec(memory_space=pl.ANY)] * 3,
        out_specs=(pl.BlockSpec(memory_space=pltpu.VMEM),) * 2,
        scratch_shapes=[
            pltpu.VMEM((NH, 2, NY, half, hidden), BF16),
            pltpu.VMEM((NH, 2, NY, half, hidden), BF16),
            pltpu.VMEM((width, hidden), BF16),
            pltpu.VMEM((frames, width), BF16),
            pltpu.VMEM((NH, 2, 2, frames, kb), BF16),
            pltpu.VMEM((2, 2, NH, 2, NL, frames, kb), BF16),
            pltpu.VMEM((kb, hidden), F32),
            pltpu.VMEM((kb, hidden), F32),
            pltpu.VMEM((kb, hidden), F32),
            pltpu.VMEM((2, 5, half, hidden), BF16),
            pltpu.VMEM((2, 2, 4, half, nk), F32),
            pltpu.VMEM((2, 4, half, nk), F32),
            pltpu.VMEM((2, 2, half, nk), F32),
            pltpu.VMEM((2, half, nk), F32),
        ]
        + [dma((n,)) for n in counts],
        compiler_params=pltpu.CompilerParams(
            collective_id=0, has_side_effects=True, vmem_limit_bytes=58 << 20
        ),
        name="grads",
    )(acts, grad_out, weight)
    return pl.pallas_call(
        finish,
        out_shape=(jax.ShapeDtypeStruct(gi.shape, BF16), jax.ShapeDtypeStruct(gw.shape, BF16)),
        in_specs=[pl.BlockSpec(memory_space=pltpu.VMEM)] * 2,
        out_specs=(pl.BlockSpec(memory_space=pl.ANY),) * 2,
        scratch_shapes=[dma((2,))],
        name="finish",
    )(pltpu.with_memory_space_constraint(gi, pltpu.VMEM), pltpu.with_memory_space_constraint(gw, pltpu.VMEM))


def solution(mesh):
    in_specs = (P(("dp", "col"), "row"), P(("dp", "row"), "col"), P("row", "col"))
    out_specs = (P(("dp", "col"), "row"), P("row", "dp", "col"))
    return jax.shard_map(shards, mesh=mesh, in_specs=in_specs, out_specs=out_specs, check_vma=False)
```

```python
import functools

import jax
import jax.numpy as jnp
from jax import lax
from jax.experimental import pallas as pl
from jax.experimental.pallas import tpu as pltpu
from jax.sharding import PartitionSpec as P

MESH = pl.DeviceIdType.MESH
F32 = jnp.float32
BF16 = jnp.bfloat16
NX = NY = NL = 4
NH = 2
NZ = NH * NL
TILE = 1024


def chunks_of(hidden):
    return [(a * hidden // 14, n * hidden // 14) for a, n in ((0, 3), (3, 4), (7, 4), (11, 3))]


class Ring:
    def __init__(self, slot, loc, me, n, dev, send_sem, recv_sem):
        self.slot, self.loc, self.dev = slot, loc, dev
        self.me = me
        self.left, self.right, self.far = (lax.rem(me + s, n) for s in (n - 1, 1, 2))
        self.sends, self.recvs = send_sem, recv_sem

    def _copy(self, ref, k, to):
        i = self.slot * 4 + k
        return pltpu.make_async_remote_copy(
            ref, ref, self.sends.at[i], self.recvs.at[i], device_id=self.dev(to), device_id_type=MESH
        )

    def _half(self, o, k):
        ref = self.loc(o)
        rows = ref.shape[0] // 2
        return ref.at[pl.ds(k * rows, rows)]

    def own(self):
        self._copy(self.loc(self.me), 0, self.right).start()
        self._copy(self.loc(self.me), 1, self.left).start()

    def from_left(self):
        self._copy(self.loc(self.left), 0, self.right).wait_recv()
        self._copy(self._half(self.left, 0), 2, self.right).start()

    def from_right(self):
        self._copy(self.loc(self.right), 1, self.left).wait_recv()
        self._copy(self._half(self.right, 1), 3, self.left).start()

    def from_far(self):
        self._copy(self._half(self.far, 0), 2, self.right).wait_recv()
        self._copy(self._half(self.far, 1), 3, self.left).wait_recv()

    def wait_sent(self):
        self._copy(self.loc(self.me), 0, self.right).wait_send()
        self._copy(self.loc(self.me), 1, self.left).wait_send()
        self._copy(self._half(self.left, 0), 2, self.right).wait_send()
        self._copy(self._half(self.right, 1), 3, self.left).wait_send()


def kernel(
    acts_hbm, grad_hbm, w_hbm, gi_ref, gw_ref,
    gp, gq, w, acts, xbuf, aall, acc, wsend, wrecv, lhs, part, pair, near, mid,
    ring_send, ring_recv, pa_send, pa_recv, loc_sem, hx_send, hx_recv, ax_send, ax_recv, az_send, az_recv,
    ac_send, ac_recv, pr_send, pr_recv, rs_send, rs_recv, ws_send, ws_recv,
):
    dp, y, col = lax.axis_index("dp"), lax.axis_index("row"), lax.axis_index("col")
    h, x, l, c = dp // NX, dp % NX, col // 2, col % 2
    z = h * NL + l
    odd = x % 2
    px = x + 1 - 2 * odd
    bx = (x + 2 * odd + NX - 1) % NX
    pbx = (px + 2 - 2 * odd + NX - 1) % NX
    half = gp.shape[3]
    kb = acts.shape[1] // NZ
    nk = part.shape[4]
    cuts = chunks_of(gp.shape[4])
    nj = len(cuts)

    def dev_x(to):
        return (h * NX + to, y, col)

    def dev_y(to):
        return (dp, to, col)

    def at_z(s):
        return lax.rem(z + s, NZ)

    def dev_z(s):
        to = at_z(s)
        return ((to // NL) * NX + x, y, (to % NL) * 2 + c)

    def side(to):
        return (to // NL + h) % 2

    pal = (dp, y, l * 2 + 1 - c)

    own_p = pltpu.make_async_copy(grad_hbm.at[pl.ds(0, half)], gp.at[0, 0, y], loc_sem.at[0])
    own_q = pltpu.make_async_copy(grad_hbm.at[pl.ds(half, half)], gq.at[0, 0, y], loc_sem.at[1])
    own_a = pltpu.make_async_copy(acts_hbm, acts, loc_sem.at[2])
    own_w = pltpu.make_async_copy(w_hbm, w, loc_sem.at[3])
    own_a.start()
    own_p.start()
    own_q.start()
    own_w.start()

    barrier = pltpu.get_barrier_semaphore()
    peers = [dev_x(px), dev_x(bx)] + [dev_y(lax.rem(y + s, NY)) for s in (1, NY - 1)]
    peers += [dev_z(s) for s in range(1, NZ)] + [pal]
    for peer in peers:
        pl.semaphore_signal(barrier, inc=1, device_id=peer, device_id_type=MESH)
    own_a.wait()
    own_p.wait()
    own_q.wait()
    pl.semaphore_wait(barrier, len(peers))

    def remote(src, dst, send, recv, i, to):
        return pltpu.make_async_remote_copy(
            src, dst, send.at[i], recv.at[i], device_id=to, device_id_type=MESH
        )

    def lanes(j):
        return pl.ds(cuts[j][0], cuts[j][1])

    class Chunk:
        def __init__(self, b, j):
            self.b, self.j, self.i = b, j, b * nj + j
            n = lanes(j)

            def ring(k, ref, s):
                return Ring(
                    k * NH * nj + self.i, lambda o: ref.at[b, s, o, :, n], y, NY, dev_y, ring_send, ring_recv
                )

            self.yq, self.y0, self.y1 = ring(0, gq, 0), ring(1, gp, 0), ring(2, gp, 1)
            self.pa = remote(
                gp.at[b, 0, y, :, n], gp.at[b, 1, y, :, n], pa_send, pa_recv, self.i * 5 + 4, dev_x(px)
            )
            self.qa = [
                remote(gq.at[b, 0, o, :, n], gq.at[b, 1, o, :, n], pa_send, pa_recv, self.i * 5 + k, dev_x(px))
                for k, o in enumerate(lax.rem(y + s, NY) for s in (0, NY - 1, 1, 2))
            ]
            self.hx = [
                remote(ref.at[0, 0, y, :, n], ref.at[1, 0, y, :, n], hx_send, hx_recv, j * 2 + k, dev_z(NL))
                for k, ref in enumerate((gp, gq))
            ]

        def byq(self):
            if self.b:
                self.hx[1].wait_recv()
            self.yq.own()

        def by0(self):
            if self.b:
                self.hx[0].wait_recv()
            self.y0.own()

        def bpa(self):
            self.pa.start()

        def bqa(self):
            self.qa[0].start()

        def mql(self):
            self.yq.from_left()
            self.qa[1].start()

        def mqr(self):
            self.yq.from_right()
            self.qa[2].start()

        def m0(self):
            self.y0.from_left()
            self.y0.from_right()

        def mp(self):
            self.pa.wait_recv()
            self.y1.own()

        def eq(self):
            self.yq.from_far()
            self.qa[3].start()

        def ep(self):
            self.y1.from_left()
            self.y1.from_right()

        def e0(self):
            self.y0.from_far()

        def dn(self):
            self.y1.from_far()
            for q in self.qa:
                q.wait_recv()

        def wait_sent(self):
            for r in (self.yq, self.y0, self.y1):
                r.wait_sent()
            for cp in self.qa + [self.pa]:
                cp.wait_send()
            if not self.b:
                for cp in self.hx:
                    cp.wait_send()

    ch = [[Chunk(b, j) for j in range(nj)] for b in range(NH)]

    ax = []
    for b in range(NH):
        for r, (theirs, mine) in enumerate(((pbx, bx), (px, x))):
            cols = pl.ds(pl.multiple_of((b * NX + theirs) * kb, kb), kb)
            ax.append(remote(acts.at[:, cols], xbuf.at[b, r, 1], ax_send, ax_recv, b * 2 + r, dev_x(px)))
            ax[-1].start()
            cols = pl.ds(pl.multiple_of((b * NX + mine) * kb, kb), kb)
            xbuf[b, r, 0] = acts[:, cols]

    def az(r, s, to):
        b = at_z(s) // NL
        return remote(
            xbuf.at[b, r], aall.at[r, c, side(to), :, to % NL], az_send, az_recv, r * NZ + s, dev_z(s)
        )

    def acts_z(r):
        for s in (4, 3, NZ - 3, 2, NZ - 2, 1, NZ - 1):
            b = at_z(s) // NL
            remote(
                xbuf.at[b, r], aall.at[r, c, (b + h) % 2, :, l], az_send, az_recv, r * NZ + s, dev_z(s)
            ).start()
        aall[r, c, 0, :, l] = xbuf[h, r]

    def ac(r, cc):
        return remote(aall.at[r, cc], aall.at[r, cc], ac_send, ac_recv, r, pal)

    def acts_core(r):
        for s in range(1, NZ):
            az(r, s, at_z(NZ - s)).wait_recv()
        ac(r, c).start()

    def wgrad(r, j):
        n = lanes(j)
        out = None
        for cc, g in enumerate((gp, gq)):
            t = lax.dot_general(
                aall[r, cc].reshape(-1, kb), g[:, :, :, :, n].reshape(-1, cuts[j][1]),
                (((0,), (0,)), ((), ())), preferred_element_type=F32,
            )
            out = t if out is None else out + t
        if r:
            acc[:, n] = out
        else:
            wsend[:, n] = out

    def ws(j):
        return remote(wsend.at[:, lanes(j)], wrecv.at[:, lanes(j)], ws_send, ws_recv, j, dev_x(bx))

    def fill():
        for d, s in enumerate((2, 0, 1, NZ - 1, NZ - 2)):
            to = at_z(s)
            lhs[0, d] = gp[side(to), 0, to % NL]
            lhs[1, d] = gq[side(to), 0, to % NL]

    def partial(k, lo, hi):
        @pl.loop(lo, hi)
        def _(t):
            cols = pl.ds(pl.multiple_of(t * TILE, TILE), TILE)
            rows = pl.ds(pl.multiple_of(k * nk + t * TILE, TILE), TILE)
            both = lhs[:, k : k + 4].reshape(8 * half, lhs.shape[3])
            r = lax.dot_general(both, w[rows], (((1,), (1,)), ((), ())), preferred_element_type=F32)
            part[:, k, :, :, cols] = r.reshape(2, 4, half, TILE)

    def pair_copy(k):
        return remote(part.at[1 - c, k], pair.at[k], pr_send, pr_recv, k, pal)

    def scatter(k):
        pair_copy(k).wait_recv()
        part[c, k] += pair[k]
        todo = (((0, 2, mid.at[0]), (2, 1, near.at[0, 0]), (3, NZ - 1, near.at[1, 0])) if k == 0 else
                ((3, NZ - 2, mid.at[1]), (1, 1, near.at[0, 1]), (2, NZ - 1, near.at[1, 1])))
        out = []
        for i, (d, s, dst) in enumerate(todo):
            out.append((k, remote(part.at[c, k, d], dst, rs_send, rs_recv, k * 3 + i, dev_z(s))))
            out[-1][1].start()
        return out

    def hx(j):
        for cp in ch[0][j].hx:
            cp.start()

    rs = []
    hx(3)
    ch[0][3].by0()
    ch[0][2].byq()
    ch[0][0].byq()
    hx(2)
    ch[0][2].bqa()
    ch[0][2].by0()
    ch[0][3].byq()
    ch[0][1].byq()
    hx(0)
    ch[0][2].bpa()
    ch[0][0].bqa()
    for cp in ax:
        cp.wait_recv()
    ch[0][2].mql()
    ch[1][3].byq()
    ch[0][0].bpa()
    ch[0][1].bpa()
    ch[0][2].m0()
    ch[0][3].mqr()
    ch[0][0].by0()
    ch[0][2].mqr()
    ch[1][3].mqr()
    ch[1][3].by0()
    ch[1][3].bqa()
    ch[1][2].byq()
    ch[0][2].mp()
    ch[0][0].mql()
    ch[0][3].bpa()
    ch[1][3].bpa()
    ch[0][2].e0()
    ch[1][3].m0()
    ch[1][2].by0()
    ch[0][1].by0()
    ch[1][2].bpa()
    acts_z(0)
    ch[1][2].mql()
    ch[0][0].mqr()
    ch[0][2].ep()
    ch[1][2].bqa()
    ch[0][2].eq()
    ch[1][0].byq()
    ch[1][3].mql()
    ch[1][2].mqr()
    ch[1][0].by0()
    ch[1][2].m0()
    ch[1][0].mqr()
    ch[1][2].mp()
    ch[0][0].m0()
    ch[1][0].m0()
    ch[0][1].m0()
    ch[1][0].bpa()
    ch[1][2].eq()
    ch[0][1].mqr()
    ch[1][0].mql()
    hx(1)
    ch[1][2].ep()
    ch[0][3].mp()
    ch[0][0].mp()
    ch[0][3].mql()
    ch[0][1].mql()
    ch[1][2].e0()
    ch[0][0].e0()
    ch[0][1].mp()
    acts_core(0)
    ch[1][0].mp()
    ch[1][0].eq()
    ch[1][0].bqa()
    ch[0][3].m0()
    ch[0][3].ep()
    ch[0][0].eq()
    ch[1][2].dn()
    ch[0][0].ep()
    ch[1][3].mp()
    ch[0][3].eq()
    ch[1][3].e0()
    ac(0, 1 - c).wait_recv()
    ch[0][2].dn()
    ch[1][0].e0()
    wgrad(0, 2)
    ws(2).start()
    ch[1][0].ep()
    ch[1][1].byq()
    acts_z(1)
    ch[1][1].by0()
    ch[0][1].bqa()
    ch[0][1].eq()
    ch[1][1].mql()
    ch[0][0].dn()
    ch[1][1].bpa()
    ch[1][1].mqr()
    ch[0][3].e0()
    ch[1][1].m0()
    ch[1][0].dn()
    ch[1][3].ep()
    wgrad(0, 0)
    ws(0).start()
    ch[0][1].e0()
    ch[1][1].eq()
    ch[0][3].bqa()
    ch[1][1].bqa()
    ch[1][3].eq()
    ch[0][1].ep()
    ch[1][1].e0()
    own_w.wait()
    fill()
    partial(1, 0, nk // TILE)
    pair_copy(1).start()
    partial(0, 0, nk // TILE)
    pair_copy(0).start()
    rs += scatter(1)
    ch[1][3].dn()
    ch[1][1].mp()
    acts_core(1)
    ch[0][3].dn()
    wgrad(0, 3)
    ws(3).start()
    ch[0][1].dn()
    ch[1][1].ep()
    ch[1][1].dn()
    wgrad(0, 1)
    ws(1).start()
    rs += scatter(0)
    ac(1, 1 - c).wait_recv()
    wgrad(1, 1)
    wgrad(1, 3)
    wgrad(1, 0)
    wgrad(1, 2)

    def gw_piece(j):
        ws(j).wait_recv()
        n = lanes(j)
        gw_ref[0, :, n] = (acc[:, n] + wrecv[:, n]).astype(BF16)

    def gi_piece(k):
        for cp in rs:
            if cp[0] == k:
                cp[1].wait_recv()
        cols = pl.ds(k * nk, nk)
        gi_ref[:, cols] = (part[c, k, 1 - k] + mid[k] + near[0, k] + near[1, k]).astype(BF16)

    for j in (2, 0):
        gw_piece(j)
    gi_piece(1)
    gw_piece(3)
    gi_piece(0)
    gw_piece(1)

    for b in range(NH):
        for j in range(nj):
            ch[b][j].wait_sent()
    for r in range(2):
        for s in range(1, NZ):
            az(r, s, z).wait_send()
        ac(r, c).wait_send()
    for j in range(nj):
        ws(j).wait_send()
    for cp in ax + [cp for _, cp in rs]:
        cp.wait_send()
    pair_copy(0).wait_send()
    pair_copy(1).wait_send()


def finish(gi_in, gw_in, gi_out, gw_out, sems):
    a = pltpu.make_async_copy(gi_in, gi_out, sems.at[0])
    b = pltpu.make_async_copy(gw_in, gw_out, sems.at[1])
    b.start()
    a.start()
    a.wait()
    b.wait()


def shards(acts, grad_out, weight):
    frames, width = acts.shape
    rows, hidden = grad_out.shape
    half = rows // 2
    kb = width // NZ
    nk = width // 2
    nj = len(chunks_of(hidden))
    dma = pltpu.SemaphoreType.DMA
    counts = [3 * NH * nj * 4] * 2 + [5 * NH * nj] * 2 + [4] + [2 * nj] * 2 + [4] * 2 + [2 * NZ] * 2
    counts += [2] * 2 + [2] * 2 + [6] * 2 + [nj] * 2
    gi, gw = pl.pallas_call(
        kernel,
        out_shape=(
            pltpu.VMEM((frames, width), BF16),
            pltpu.VMEM((1, kb, hidden), BF16),
        ),
        in_specs=[pl.BlockSpec(memory_space=pl.ANY)] * 3,
        out_specs=(pl.BlockSpec(memory_space=pltpu.VMEM),) * 2,
        scratch_shapes=[
            pltpu.VMEM((NH, 2, NY, half, hidden), BF16),
            pltpu.VMEM((NH, 2, NY, half, hidden), BF16),
            pltpu.VMEM((width, hidden), BF16),
            pltpu.VMEM((frames, width), BF16),
            pltpu.VMEM((NH, 2, 2, frames, kb), BF16),
            pltpu.VMEM((2, 2, NH, 2, NL, frames, kb), BF16),
            pltpu.VMEM((kb, hidden), F32),
            pltpu.VMEM((kb, hidden), F32),
            pltpu.VMEM((kb, hidden), F32),
            pltpu.VMEM((2, 5, half, hidden), BF16),
            pltpu.VMEM((2, 2, 4, half, nk), F32),
            pltpu.VMEM((2, 4, half, nk), F32),
            pltpu.VMEM((2, 2, half, nk), F32),
            pltpu.VMEM((2, half, nk), F32),
        ]
        + [dma((n,)) for n in counts],
        compiler_params=pltpu.CompilerParams(
            collective_id=0, has_side_effects=True, vmem_limit_bytes=58 << 20
        ),
        name="grads",
    )(acts, grad_out, weight)
    return pl.pallas_call(
        finish,
        out_shape=(jax.ShapeDtypeStruct(gi.shape, BF16), jax.ShapeDtypeStruct(gw.shape, BF16)),
        in_specs=[pl.BlockSpec(memory_space=pltpu.VMEM)] * 2,
        out_specs=(pl.BlockSpec(memory_space=pl.ANY),) * 2,
        scratch_shapes=[dma((2,))],
        name="finish",
    )(pltpu.with_memory_space_constraint(gi, pltpu.VMEM), pltpu.with_memory_space_constraint(gw, pltpu.VMEM))


def solution(mesh):
    in_specs = (P(("dp", "col"), "row"), P(("dp", "row"), "col"), P("row", "col"))
    out_specs = (P(("dp", "col"), "row"), P("row", "dp", "col"))
    return jax.shard_map(shards, mesh=mesh, in_specs=in_specs, out_specs=out_specs, check_vma=False)
```

```python
import functools

import jax
import jax.numpy as jnp
from jax import lax
from jax.experimental import pallas as pl
from jax.experimental.pallas import tpu as pltpu
from jax.sharding import PartitionSpec as P

MESH = pl.DeviceIdType.MESH
F32 = jnp.float32
BF16 = jnp.bfloat16
NX = NY = NL = 4
NH = 2
NZ = NH * NL
TILE = 1024


def chunks_of(hidden):
    return [(a * hidden // 14, n * hidden // 14) for a, n in ((0, 3), (3, 4), (7, 4), (11, 3))]


class Ring:
    def __init__(self, slot, loc, me, n, dev, send_sem, recv_sem):
        self.slot, self.loc, self.dev = slot, loc, dev
        self.me = me
        self.left, self.right, self.far = (lax.rem(me + s, n) for s in (n - 1, 1, 2))
        self.sends, self.recvs = send_sem, recv_sem

    def _copy(self, ref, k, to):
        i = self.slot * 4 + k
        return pltpu.make_async_remote_copy(
            ref, ref, self.sends.at[i], self.recvs.at[i], device_id=self.dev(to), device_id_type=MESH
        )

    def _half(self, o, k):
        ref = self.loc(o)
        rows = ref.shape[0] // 2
        return ref.at[pl.ds(k * rows, rows)]

    def own(self):
        self._copy(self.loc(self.me), 0, self.right).start()
        self._copy(self.loc(self.me), 1, self.left).start()

    def from_left(self):
        self._copy(self.loc(self.left), 0, self.right).wait_recv()
        self._copy(self._half(self.left, 0), 2, self.right).start()

    def from_right(self):
        self._copy(self.loc(self.right), 1, self.left).wait_recv()
        self._copy(self._half(self.right, 1), 3, self.left).start()

    def from_far(self):
        self._copy(self._half(self.far, 0), 2, self.right).wait_recv()
        self._copy(self._half(self.far, 1), 3, self.left).wait_recv()

    def wait_sent(self):
        self._copy(self.loc(self.me), 0, self.right).wait_send()
        self._copy(self.loc(self.me), 1, self.left).wait_send()
        self._copy(self._half(self.left, 0), 2, self.right).wait_send()
        self._copy(self._half(self.right, 1), 3, self.left).wait_send()


def kernel(
    acts_hbm, grad_hbm, w_hbm, gi_ref, gw_ref,
    gp, gq, w, acts, xbuf, aall, acc, wsend, wrecv, lhs, part, pair, near, mid,
    ring_send, ring_recv, pa_send, pa_recv, loc_sem, hx_send, hx_recv, ax_send, ax_recv, az_send, az_recv,
    ac_send, ac_recv, pr_send, pr_recv, rs_send, rs_recv, ws_send, ws_recv,
):
    dp, y, col = lax.axis_index("dp"), lax.axis_index("row"), lax.axis_index("col")
    h, x, l, c = dp // NX, dp % NX, col // 2, col % 2
    z = h * NL + l
    odd = x % 2
    px = x + 1 - 2 * odd
    bx = (x + 2 * odd + NX - 1) % NX
    pbx = (px + 2 - 2 * odd + NX - 1) % NX
    half = gp.shape[3]
    kb = acts.shape[1] // NZ
    nk = part.shape[4]
    cuts = chunks_of(gp.shape[4])
    nj = len(cuts)

    def dev_x(to):
        return (h * NX + to, y, col)

    def dev_y(to):
        return (dp, to, col)

    def at_z(s):
        return lax.rem(z + s, NZ)

    def dev_z(s):
        to = at_z(s)
        return ((to // NL) * NX + x, y, (to % NL) * 2 + c)

    def side(to):
        return (to // NL + h) % 2

    pal = (dp, y, l * 2 + 1 - c)

    own_p = pltpu.make_async_copy(grad_hbm.at[pl.ds(0, half)], gp.at[0, 0, y], loc_sem.at[0])
    own_q = pltpu.make_async_copy(grad_hbm.at[pl.ds(half, half)], gq.at[0, 0, y], loc_sem.at[1])
    own_a = pltpu.make_async_copy(acts_hbm, acts, loc_sem.at[2])
    own_w = pltpu.make_async_copy(w_hbm, w, loc_sem.at[3])
    own_a.start()
    own_p.start()
    own_q.start()
    own_w.start()

    barrier = pltpu.get_barrier_semaphore()
    peers = [dev_x(px), dev_x(bx)] + [dev_y(lax.rem(y + s, NY)) for s in (1, NY - 1)]
    peers += [dev_z(s) for s in range(1, NZ)] + [pal]
    for peer in peers:
        pl.semaphore_signal(barrier, inc=1, device_id=peer, device_id_type=MESH)
    own_a.wait()
    own_p.wait()
    own_q.wait()
    pl.semaphore_wait(barrier, len(peers))

    def remote(src, dst, send, recv, i, to):
        return pltpu.make_async_remote_copy(
            src, dst, send.at[i], recv.at[i], device_id=to, device_id_type=MESH
        )

    def lanes(j):
        return pl.ds(cuts[j][0], cuts[j][1])

    class Chunk:
        def __init__(self, b, j):
            self.b, self.j, self.i = b, j, b * nj + j
            n = lanes(j)

            def ring(k, ref, s):
                return Ring(
                    k * NH * nj + self.i, lambda o: ref.at[b, s, o, :, n], y, NY, dev_y, ring_send, ring_recv
                )

            self.yq, self.y0, self.y1 = ring(0, gq, 0), ring(1, gp, 0), ring(2, gp, 1)
            self.pa = remote(
                gp.at[b, 0, y, :, n], gp.at[b, 1, y, :, n], pa_send, pa_recv, self.i * 5 + 4, dev_x(px)
            )
            self.qa = [
                remote(gq.at[b, 0, o, :, n], gq.at[b, 1, o, :, n], pa_send, pa_recv, self.i * 5 + k, dev_x(px))
                for k, o in enumerate(lax.rem(y + s, NY) for s in (0, NY - 1, 1, 2))
            ]
            self.hx = [
                remote(ref.at[0, 0, y, :, n], ref.at[1, 0, y, :, n], hx_send, hx_recv, j * 2 + k, dev_z(NL))
                for k, ref in enumerate((gp, gq))
            ]

        def byq(self):
            if self.b:
                self.hx[1].wait_recv()
            self.yq.own()

        def by0(self):
            if self.b:
                self.hx[0].wait_recv()
            self.y0.own()

        def bpa(self):
            self.pa.start()

        def bqa(self):
            self.qa[0].start()

        def mql(self):
            self.yq.from_left()
            self.qa[1].start()

        def mqr(self):
            self.yq.from_right()
            self.qa[2].start()

        def m0(self):
            self.y0.from_left()
            self.y0.from_right()

        def mp(self):
            self.pa.wait_recv()
            self.y1.own()

        def eq(self):
            self.yq.from_far()
            self.qa[3].start()

        def ep(self):
            self.y1.from_left()
            self.y1.from_right()

        def e0(self):
            self.y0.from_far()

        def dn(self):
            self.y1.from_far()
            for q in self.qa:
                q.wait_recv()

        def wait_sent(self):
            for r in (self.yq, self.y0, self.y1):
                r.wait_sent()
            for cp in self.qa + [self.pa]:
                cp.wait_send()
            if not self.b:
                for cp in self.hx:
                    cp.wait_send()

    ch = [[Chunk(b, j) for j in range(nj)] for b in range(NH)]

    ax = []
    for b in range(NH):
        for r, (theirs, mine) in enumerate(((pbx, bx), (px, x))):
            cols = pl.ds(pl.multiple_of((b * NX + theirs) * kb, kb), kb)
            ax.append(remote(acts.at[:, cols], xbuf.at[b, r, 1], ax_send, ax_recv, b * 2 + r, dev_x(px)))
            ax[-1].start()
            cols = pl.ds(pl.multiple_of((b * NX + mine) * kb, kb), kb)
            xbuf[b, r, 0] = acts[:, cols]

    def az(r, s, to):
        b = at_z(s) // NL
        return remote(
            xbuf.at[b, r], aall.at[r, c, side(to), :, to % NL], az_send, az_recv, r * NZ + s, dev_z(s)
        )

    def acts_z(r):
        for s in (4, 3, NZ - 3, 2, NZ - 2, 1, NZ - 1):
            b = at_z(s) // NL
            remote(
                xbuf.at[b, r], aall.at[r, c, (b + h) % 2, :, l], az_send, az_recv, r * NZ + s, dev_z(s)
            ).start()
        aall[r, c, 0, :, l] = xbuf[h, r]

    def ac(r, cc):
        return remote(aall.at[r, cc], aall.at[r, cc], ac_send, ac_recv, r, pal)

    def acts_core(r):
        for s in range(1, NZ):
            az(r, s, at_z(NZ - s)).wait_recv()
        ac(r, c).start()

    def wgrad(r, j):
        n = lanes(j)
        out = None
        for cc, g in enumerate((gp, gq)):
            t = lax.dot_general(
                aall[r, cc].reshape(-1, kb), g[:, :, :, :, n].reshape(-1, cuts[j][1]),
                (((0,), (0,)), ((), ())), preferred_element_type=F32,
            )
            out = t if out is None else out + t
        if r:
            acc[:, n] = out
        else:
            wsend[:, n] = out

    def ws(j):
        return remote(wsend.at[:, lanes(j)], wrecv.at[:, lanes(j)], ws_send, ws_recv, j, dev_x(bx))

    def fill():
        for d, s in enumerate((2, 0, 1, NZ - 1, NZ - 2)):
            to = at_z(s)
            lhs[0, d] = gp[side(to), 0, to % NL]
            lhs[1, d] = gq[side(to), 0, to % NL]

    def partial(k, lo, hi):
        @pl.loop(lo, hi)
        def _(t):
            cols = pl.ds(pl.multiple_of(t * TILE, TILE), TILE)
            rows = pl.ds(pl.multiple_of(k * nk + t * TILE, TILE), TILE)
            both = lhs[:, k : k + 4].reshape(8 * half, lhs.shape[3])
            r = lax.dot_general(both, w[rows], (((1,), (1,)), ((), ())), preferred_element_type=F32)
            part[:, k, :, :, cols] = r.reshape(2, 4, half, TILE)

    def pair_copy(k):
        return remote(part.at[1 - c, k], pair.at[k], pr_send, pr_recv, k, pal)

    def scatter(k):
        pair_copy(k).wait_recv()
        part[c, k] += pair[k]
        todo = (((0, 2, mid.at[0]), (2, 1, near.at[0, 0]), (3, NZ - 1, near.at[1, 0])) if k == 0 else
                ((3, NZ - 2, mid.at[1]), (1, 1, near.at[0, 1]), (2, NZ - 1, near.at[1, 1])))
        out = []
        for i, (d, s, dst) in enumerate(todo):
            out.append((k, remote(part.at[c, k, d], dst, rs_send, rs_recv, k * 3 + i, dev_z(s))))
            out[-1][1].start()
        return out

    def hx(j):
        for cp in ch[0][j].hx[::-1]:
            cp.start()

    rs = []
    hx(3)
    ch[0][3].by0()
    ch[0][2].byq()
    ch[0][0].byq()
    hx(2)
    ch[0][2].bqa()
    ch[0][2].by0()
    ch[0][3].byq()
    ch[0][1].byq()
    hx(0)
    ch[0][2].bpa()
    ch[0][0].bqa()
    for cp in ax:
        cp.wait_recv()
    ch[0][2].mql()
    ch[1][3].byq()
    ch[0][0].bpa()
    ch[0][1].bpa()
    ch[0][2].m0()
    ch[0][3].mqr()
    ch[0][0].by0()
    ch[0][2].mqr()
    ch[1][3].mqr()
    ch[1][3].by0()
    ch[1][3].bqa()
    ch[1][2].byq()
    ch[0][2].mp()
    ch[0][0].mql()
    ch[0][3].bpa()
    ch[1][3].bpa()
    ch[0][2].e0()
    ch[1][3].m0()
    ch[1][2].by0()
    ch[0][1].by0()
    ch[1][2].bpa()
    acts_z(0)
    ch[1][2].mql()
    ch[0][0].mqr()
    ch[0][2].ep()
    ch[1][2].bqa()
    ch[0][2].eq()
    ch[1][0].byq()
    ch[1][3].mql()
    ch[1][2].mqr()
    ch[1][0].by0()
    ch[1][2].m0()
    ch[1][0].mqr()
    ch[1][2].mp()
    ch[0][0].m0()
    ch[1][0].m0()
    ch[0][1].m0()
    ch[1][0].bpa()
    ch[1][2].eq()
    ch[0][1].mqr()
    ch[1][0].mql()
    hx(1)
    ch[1][2].ep()
    ch[0][3].mp()
    ch[0][0].mp()
    ch[0][3].mql()
    ch[0][1].mql()
    ch[1][2].e0()
    ch[0][0].e0()
    ch[0][1].mp()
    acts_core(0)
    ch[1][0].mp()
    ch[1][0].eq()
    ch[1][0].bqa()
    ch[0][3].m0()
    ch[0][3].ep()
    ch[0][0].eq()
    ch[1][2].dn()
    ch[0][0].ep()
    ch[1][3].mp()
    ch[0][3].eq()
    ch[1][3].e0()
    ac(0, 1 - c).wait_recv()
    ch[0][2].dn()
    ch[1][0].e0()
    wgrad(0, 2)
    ws(2).start()
    ch[1][0].ep()
    ch[1][1].byq()
    acts_z(1)
    ch[1][1].by0()
    ch[0][1].bqa()
    ch[0][1].eq()
    ch[1][1].mql()
    ch[0][0].dn()
    ch[1][1].bpa()
    ch[1][1].mqr()
    ch[0][3].e0()
    ch[1][1].m0()
    ch[1][0].dn()
    ch[1][3].ep()
    wgrad(0, 0)
    ws(0).start()
    ch[0][1].e0()
    ch[1][1].eq()
    ch[0][3].bqa()
    ch[1][1].bqa()
    ch[1][3].eq()
    ch[0][1].ep()
    ch[1][1].e0()
    own_w.wait()
    fill()
    partial(1, 0, nk // TILE)
    pair_copy(1).start()
    partial(0, 0, nk // TILE)
    pair_copy(0).start()
    rs += scatter(1)
    ch[1][3].dn()
    ch[1][1].mp()
    acts_core(1)
    ch[0][3].dn()
    wgrad(0, 3)
    ws(3).start()
    ch[0][1].dn()
    ch[1][1].ep()
    ch[1][1].dn()
    wgrad(0, 1)
    ws(1).start()
    rs += scatter(0)
    ac(1, 1 - c).wait_recv()
    wgrad(1, 1)
    wgrad(1, 3)
    wgrad(1, 0)
    wgrad(1, 2)

    def gw_piece(j):
        ws(j).wait_recv()
        n = lanes(j)
        gw_ref[0, :, n] = (acc[:, n] + wrecv[:, n]).astype(BF16)

    def gi_piece(k):
        for cp in rs:
            if cp[0] == k:
                cp[1].wait_recv()
        cols = pl.ds(k * nk, nk)
        gi_ref[:, cols] = (part[c, k, 1 - k] + mid[k] + near[0, k] + near[1, k]).astype(BF16)

    for j in (2, 0):
        gw_piece(j)
    gi_piece(1)
    gw_piece(3)
    gi_piece(0)
    gw_piece(1)

    for b in range(NH):
        for j in range(nj):
            ch[b][j].wait_sent()
    for r in range(2):
        for s in range(1, NZ):
            az(r, s, z).wait_send()
        ac(r, c).wait_send()
    for j in range(nj):
        ws(j).wait_send()
    for cp in ax + [cp for _, cp in rs]:
        cp.wait_send()
    pair_copy(0).wait_send()
    pair_copy(1).wait_send()


def finish(gi_in, gw_in, gi_out, gw_out, sems):
    a = pltpu.make_async_copy(gi_in, gi_out, sems.at[0])
    b = pltpu.make_async_copy(gw_in, gw_out, sems.at[1])
    b.start()
    a.start()
    a.wait()
    b.wait()


def shards(acts, grad_out, weight):
    frames, width = acts.shape
    rows, hidden = grad_out.shape
    half = rows // 2
    kb = width // NZ
    nk = width // 2
    nj = len(chunks_of(hidden))
    dma = pltpu.SemaphoreType.DMA
    counts = [3 * NH * nj * 4] * 2 + [5 * NH * nj] * 2 + [4] + [2 * nj] * 2 + [4] * 2 + [2 * NZ] * 2
    counts += [2] * 2 + [2] * 2 + [6] * 2 + [nj] * 2
    gi, gw = pl.pallas_call(
        kernel,
        out_shape=(
            pltpu.VMEM((frames, width), BF16),
            pltpu.VMEM((1, kb, hidden), BF16),
        ),
        in_specs=[pl.BlockSpec(memory_space=pl.ANY)] * 3,
        out_specs=(pl.BlockSpec(memory_space=pltpu.VMEM),) * 2,
        scratch_shapes=[
            pltpu.VMEM((NH, 2, NY, half, hidden), BF16),
            pltpu.VMEM((NH, 2, NY, half, hidden), BF16),
            pltpu.VMEM((width, hidden), BF16),
            pltpu.VMEM((frames, width), BF16),
            pltpu.VMEM((NH, 2, 2, frames, kb), BF16),
            pltpu.VMEM((2, 2, NH, 2, NL, frames, kb), BF16),
            pltpu.VMEM((kb, hidden), F32),
            pltpu.VMEM((kb, hidden), F32),
            pltpu.VMEM((kb, hidden), F32),
            pltpu.VMEM((2, 5, half, hidden), BF16),
            pltpu.VMEM((2, 2, 4, half, nk), F32),
            pltpu.VMEM((2, 4, half, nk), F32),
            pltpu.VMEM((2, 2, half, nk), F32),
            pltpu.VMEM((2, half, nk), F32),
        ]
        + [dma((n,)) for n in counts],
        compiler_params=pltpu.CompilerParams(
            collective_id=0, has_side_effects=True, vmem_limit_bytes=58 << 20
        ),
        name="grads",
    )(acts, grad_out, weight)
    return pl.pallas_call(
        finish,
        out_shape=(jax.ShapeDtypeStruct(gi.shape, BF16), jax.ShapeDtypeStruct(gw.shape, BF16)),
        in_specs=[pl.BlockSpec(memory_space=pltpu.VMEM)] * 2,
        out_specs=(pl.BlockSpec(memory_space=pl.ANY),) * 2,
        scratch_shapes=[dma((2,))],
        name="finish",
    )(pltpu.with_memory_space_constraint(gi, pltpu.VMEM), pltpu.with_memory_space_constraint(gw, pltpu.VMEM))


def solution(mesh):
    in_specs = (P(("dp", "col"), "row"), P(("dp", "row"), "col"), P("row", "col"))
    out_specs = (P(("dp", "col"), "row"), P("row", "dp", "col"))
    return jax.shard_map(shards, mesh=mesh, in_specs=in_specs, out_specs=out_specs, check_vma=False)
```
